256 devices in a mesh: dp: 8 (over z_hi, x), expert: 32 (over y, z_lo, core).
Axes of the slice: x: 4, y: 4, z: 8 (z_hi: 2, z_lo: 4; z = z_hi * 4 + z_lo), core: 2. Of those that a mesh axis runs over, the one named last changes fastest.
Arguments:
- tokens: bfloat16 [4096, 3584], P('expert'), may hold values from -6 to 6
- expert_ids: int32 [4096, 8], P('expert'), may hold values from 0 to 31, all different within a row; in each aligned block of 128 rows (0 to 127, 128 to 255, ...) at most 48 rows name the same one
- route_weight: float32 [4096, 8], P('expert'), may hold values from 0.1 to 1
- pair_swap: int32 [16], replicated, may hold values from 0 to 1, as said below
- expert_gate: bfloat16 [32, 3584, 2048], P('expert', None, 'dp'), may hold values from -0.09375 to 0.09375
- expert_up: bfloat16 [32, 3584, 2048], P('expert', None, 'dp'), may hold values from -0.09375 to 0.09375
- expert_down: bfloat16 [32, 2048, 3584], P('expert', 'dp'), may hold values from -0.1875 to 0.1875
- shared_gate: bfloat16 [3584, 2048], P(None, 'dp'), may hold values from -0.09375 to 0.09375
- shared_up: bfloat16 [3584, 2048], P(None, 'dp'), may hold values from -0.09375 to 0.09375
- shared_down: bfloat16 [2048, 3584], P('dp'), may hold values from -0.1875 to 0.1875
Outputs:
- layer_out: bfloat16 [4096, 3584], P('expert', 'dp')
The draws below stay inside these ranges and needn't reach their ends.
Inputs may be any that keep to these rules, and one draw needn't show every extreme that they name: `expert_ids`: each row names 8 different experts; within the rows of one device (aligned blocks of 128 rows) no expert is named more than 48 times, a bound that some block reaches. `pair_swap`: entry 0 is always 1; the other entries are 0 or 1.
All inputs are finite; a program needn't handle non-finite values.
Results may differ from the reference program's by a relative error of at most 0.012.
Values may be sent and summed in bfloat16 or wider, within the bound.
A program may use at most 192 MiB of HBM per device.

```python
import math
import jax
import jax.numpy as jnp
import numpy as np
from jax import lax

D = 3584
HIDDEN_SIZE = 2048
TOPK = 8
TOK_DEV = 128
EXPERTS = 32
HID_DEV = 256
MOST = 48
TOKENS = 4096
N_DP = 8
N_EXPERT = 32


def draw_pair_swap(key, part):
    flags = jax.random.randint(key, (EXPERTS // 2,), 0, 2).astype(jnp.int32)
    return flags.at[0].set(1)


def spiked(result, own_key, source, target, shards_of, factor):
    def block_of(dim):
        return (jnp.arange(result.shape[dim]) // (result.shape[dim] // shards_of)).reshape((-1,) + (1,) * (result.ndim - 1 - dim))

    first = jax.random.permutation(own_key, shards_of)[block_of(target)]
    second = (block_of(target) + shards_of // 2) % shards_of
    return jnp.where((block_of(source) == first) | (block_of(source) == second), factor * result, result)


def block_levels(rng, shape, cuts, smallest, high):
    def one(axis_at, blocks):
        steps = jax.random.uniform(jax.random.fold_in(jax.random.fold_in(rng, 6), axis_at), (blocks,), jnp.float32, smallest / len(cuts), high / len(cuts))
        return jnp.repeat(jnp.exp(steps), shape[axis_at] // blocks).reshape((-1,) + (1,) * (len(shape) - axis_at - 1))

    factor_of = one(*cuts[0])
    for cut in cuts[1:]:
        factor_of = factor_of * one(*cut)
    return factor_of


def assign_block(own_key, own, number, rows, number_of, top, reach, slope):
    order = jax.random.permutation(own_key, number_of)
    crowded, ordinary = load_shares(number_of, rows * top, reach, slope, True), load_shares(number_of, rows * top, reach, slope, False)
    places = jnp.arange(number_of)

    def named(lengths, rotation):
        used = int((lengths > 0).sum())
        fixed = max(1, used // 4)
        passed = fixed + (places - fixed + rotation * (used - fixed)) % max(1, number_of - fixed)
        return jnp.zeros((number_of,), jnp.int32).at[order[jnp.where(places < fixed, places, passed)]].set(jnp.asarray(lengths, jnp.int32))

    lengths = jnp.where(number % 4 == 0, named(crowded, number // 4), named(ordinary, number - number // 4 - 1))
    mixed = jax.random.permutation(jax.random.fold_in(own, 3), number_of)
    giver, receiver = mixed[0:number_of // 2 * 2:2], mixed[1:number_of // 2 * 2:2]
    slack = jnp.minimum(lengths[giver] - 1, reach - lengths[receiver]) // 2
    slack = jnp.where((giver == order[0]) | (receiver == order[0]) | (lengths[receiver] == 0), 0, jnp.maximum(slack, 0))
    passed = jax.random.randint(jax.random.fold_in(own, 4), (number_of // 2,), 0, 1 << 20) % (slack + 1)
    lengths = lengths.at[giver].add(-passed).at[receiver].add(passed)
    labels = jnp.searchsorted(jnp.cumsum(lengths), jnp.arange(rows * top), side="right").astype(jnp.int32)
    listing = labels.reshape(top, rows).T
    listing = listing[jax.random.permutation(jax.random.fold_in(own, 1), rows)]
    rotation = jax.random.randint(jax.random.fold_in(own, 2), (rows, 1), 0, top)
    return jnp.take_along_axis(listing, (jnp.arange(top)[None, :] + rotation) % top, axis=1)


def load_shares(count, total, most, slope, full):
    portions = [(1 << 20) // math.isqrt(rank ** slope) + 1 for rank in range(1, count + 1)]
    largest = most if full else min(most, max(-(-total // count), total * portions[0] // sum(portions)))
    least = 1 if total - largest >= count - 1 else 0
    counts, surplus = [largest] + [least] * (count - 1), total - largest - least * (count - 1)
    while surplus > 0:
        free = [i for i in range(1, count) if counts[i] < largest] or [i for i in range(1, count) if counts[i] < most]
        whole, remaining = sum([portions[i] for i in free]), surplus
        for i in free:
            extra = min(most - counts[i], max(1, remaining * portions[i] // whole), surplus)
            counts[i] = counts[i] + extra
            surplus = surplus - extra
    return np.array(counts)


def centred(key, shape, scale, limit, shards=(), held_as=jnp.bfloat16):
    result = scale * jax.random.normal(key, shape, jnp.float32)
    if shards:
        result = result * block_levels(key, shape, shards, -0.22, 0.18)
    return jnp.clip(result, -limit, limit).astype(held_as)


def gaussian_with(own_key, shape, width, limit, cuts, heavy, kind=jnp.bfloat16):
    result = width * jax.random.normal(own_key, shape, jnp.float32)
    if cuts:
        result = result * block_levels(own_key, shape, cuts, -0.22, 0.18)
    return jnp.clip(spiked(result, jax.random.fold_in(own_key, 3), *heavy), -limit, limit).astype(kind)


def setup_inputs(seed: int = 0) -> dict:
    arg_keys = jax.random.split(jax.random.key(seed), 11)
    tokens = centred(arg_keys[0], (TOKENS, D), 1.0, 6.0, ((0, 32),))
    expert_ids_keys = jax.random.split(jax.random.fold_in(arg_keys[1], 1), TOKENS // TOK_DEV)
    expert_ids_turns = jax.random.permutation(jax.random.fold_in(arg_keys[1], 3), TOKENS // TOK_DEV)
    expert_ids = jax.vmap(lambda own, number: assign_block(jax.random.fold_in(arg_keys[1], 2), own, number, TOK_DEV, EXPERTS, TOPK, MOST, 2))(expert_ids_keys, expert_ids_turns).reshape((TOKENS, TOPK))
    route_weight = jnp.clip(jnp.exp(math.log(1.0) - 2.3025851 * jax.random.uniform(arg_keys[2], (TOKENS, TOPK), jnp.float32) ** block_levels(arg_keys[2], (TOKENS, TOPK), ((0, 32),), -0.2, 0.2)), 0.1, 1.0)
    pair_swap = draw_pair_swap(jax.random.fold_in(arg_keys[10], 71), 0)
    expert_gate = centred(arg_keys[4], (EXPERTS, D, HIDDEN_SIZE), D ** -0.5, 0.09375, ((0, 32), (2, 8)))
    expert_up = centred(arg_keys[5], (EXPERTS, D, HIDDEN_SIZE), D ** -0.5, 0.09375, ((0, 32), (2, 8)))
    expert_down = gaussian_with(arg_keys[6], (EXPERTS, HIDDEN_SIZE, D), HIDDEN_SIZE ** -0.5, 0.1875, ((0, 32), (1, 8)), (1, 2, 8, 2.0))
    shared_gate = centred(arg_keys[7], (D, HIDDEN_SIZE), D ** -0.5, 0.09375, ((1, 8),))
    shared_up = centred(arg_keys[8], (D, HIDDEN_SIZE), D ** -0.5, 0.09375, ((1, 8),))
    shared_down = gaussian_with(arg_keys[9], (HIDDEN_SIZE, D), HIDDEN_SIZE ** -0.5, 0.1875, ((0, 8),), (0, 1, 8, 2.0))
    return {"tokens": tokens, "expert_ids": expert_ids, "route_weight": route_weight, "pair_swap": pair_swap, "expert_gate": expert_gate, "expert_up": expert_up, "expert_down": expert_down, "shared_gate": shared_gate, "shared_up": shared_up, "shared_down": shared_down}


def reference(tokens, expert_ids, route_weight, pair_swap, expert_gate, expert_up, expert_down, shared_gate, shared_up, shared_down):
    half_axis = EXPERTS // 2
    columns = jnp.arange(EXPERTS, dtype=jnp.int32)
    swap_flags = pair_swap[columns % half_axis]
    holder = jnp.where(swap_flags == 1, (columns + half_axis) % EXPERTS, columns).astype(jnp.int32)
    mix = route_weight / jnp.sum(route_weight, axis=1, keepdims=True)
    shared_gv = jnp.dot(tokens, shared_gate, preferred_element_type=jnp.float32)
    shared_uv = jnp.dot(tokens, shared_up, preferred_element_type=jnp.float32)
    shared_act = (jax.nn.silu(shared_gv) * shared_uv).astype(jnp.bfloat16)
    shared_out = jnp.dot(shared_act, shared_down, preferred_element_type=jnp.float32)
    flat_ids = expert_ids.reshape(-1)
    flat_mix = mix.reshape(-1)
    owner_row = (jnp.arange(TOKENS * TOPK, dtype=jnp.int32) // TOPK).astype(jnp.int32)
    capacity = N_EXPERT * MOST
    padded = jnp.concatenate([tokens, jnp.zeros((1, D), tokens.dtype)], axis=0)

    def accumulate(carry, expert):
        stored = holder[expert]
        chosen = (flat_ids == expert).astype(jnp.int32)
        before = jnp.cumsum(chosen) - chosen
        position = jnp.where(chosen == 1, before, capacity).astype(jnp.int32)
        rows_at = jnp.full((capacity + 1,), TOKENS, jnp.int32).at[position].set(owner_row)[:capacity]
        mix_at = jnp.zeros((capacity + 1,), jnp.float32).at[position].set(flat_mix)[:capacity]
        rows_in = padded[rows_at]
        gate_val = jnp.dot(rows_in, expert_gate[stored], preferred_element_type=jnp.float32)
        up_val = jnp.dot(rows_in, expert_up[stored], preferred_element_type=jnp.float32)
        act = (jax.nn.silu(gate_val) * up_val).astype(jnp.bfloat16)
        act_groups = act.reshape(capacity, N_DP, HID_DEV).astype(jnp.float32)
        down_groups = expert_down[stored].reshape(N_DP, HID_DEV, D).astype(jnp.float32)
        parts = jnp.einsum("cnh,nhd->ncd", act_groups, down_groups).astype(jnp.bfloat16)
        parts = lax.optimization_barrier(parts)
        summed = jnp.sum(parts.astype(jnp.float32), axis=0)
        carry = carry.at[rows_at].add(mix_at[:, None] * summed)
        return carry, None

    start = jnp.zeros((TOKENS + 1, D), jnp.float32)
    routed, _ = lax.scan(accumulate, start, jnp.arange(EXPERTS, dtype=jnp.int32))
    return (shared_out + 2.5 * routed[:TOKENS]).astype(jnp.bfloat16)
```

```python
import jax
import jax.numpy as jnp
from jax import lax
from jax.sharding import PartitionSpec as P

routed_scale = 2.5


def local(
    tokens,
    expert_ids,
    route_weight,
    pair_swap,
    expert_gate,
    expert_up,
    expert_down,
    shared_gate,
    shared_up,
    shared_down,
):
    f32 = jnp.float32
    rows = tokens.shape[0]
    experts = lax.axis_size("expert")
    half = experts // 2
    columns = jnp.arange(experts, dtype=jnp.int32)
    swap = jnp.concatenate([pair_swap, pair_swap])
    stored = jnp.where(swap == 1, (columns + half) % experts, columns)
    mix = route_weight / jnp.sum(route_weight, axis=1, keepdims=True)
    dense = jnp.sum(
        jnp.where(expert_ids[:, :, None] == stored[None, None, :], routed_scale * mix[:, :, None], 0.0), axis=1
    )
    every = lax.all_gather(tokens, "expert", axis=0, tiled=True)
    mine = lax.all_to_all(dense, "expert", split_axis=1, concat_axis=0, tiled=True)
    gate_val = jnp.dot(every, expert_gate[0], preferred_element_type=f32)
    up_val = jnp.dot(every, expert_up[0], preferred_element_type=f32)
    act = (jax.nn.silu(gate_val) * up_val * mine).astype(jnp.bfloat16)
    part = jnp.dot(act, expert_down[0], preferred_element_type=f32)
    shared_gv = jnp.dot(tokens, shared_gate, preferred_element_type=f32)
    shared_uv = jnp.dot(tokens, shared_up, preferred_element_type=f32)
    shared_act = (jax.nn.silu(shared_gv) * shared_uv).astype(jnp.bfloat16)
    shared_out = jnp.dot(shared_act, shared_down, preferred_element_type=f32)
    first = lax.psum_scatter(part.astype(jnp.bfloat16), "dp", scatter_dimension=1, tiled=True)
    second = lax.psum_scatter(first, "expert", scatter_dimension=0, tiled=True)
    shared_sum = lax.psum_scatter(shared_out.astype(jnp.bfloat16), "dp", scatter_dimension=1, tiled=True)
    return (second.astype(f32) + shared_sum.astype(f32)).astype(jnp.bfloat16)


def solution(mesh):
    in_specs = (
        P("expert", None),
        P("expert", None),
        P("expert", None),
        P(),
        P("expert", None, "dp"),
        P("expert", None, "dp"),
        P("expert", "dp", None),
        P(None, "dp"),
        P(None, "dp"),
        P("dp", None),
    )
    return jax.shard_map(local, mesh=mesh, in_specs=in_specs, out_specs=P("expert", "dp"), check_vma=False)
```

```python
import functools

import jax
import jax.numpy as jnp
from jax import lax
from jax.experimental import pallas as pl
from jax.experimental.pallas import tpu as pltpu
from jax.sharding import PartitionSpec as P

MESH = pl.DeviceIdType.MESH
F32 = jnp.float32
BF16 = jnp.bfloat16
routed_scale = 2.5
D = 3584
TOK = 128
HID = 256
C1 = (0, 896)
C2 = (896, 1152)
QBASE, QW = 2048, 384
ROWS = (48, 48, 32)
OFFS = (0, 48, 96)
XC = 896
SPLIT = (32, 32, 16)


class Place:
    def __init__(self):
        self.dp = lax.axis_index("dp")
        self.ex = lax.axis_index("expert")
        self.x = self.dp % 4
        self.zh = self.dp // 4
        self.y = self.ex // 8
        self.k = (self.ex // 2) % 4
        self.c = self.ex % 2
        self.z = self.zh * 4 + self.k

    def xn(self, d):
        return (self.zh * 4 + (self.x + d + 4) % 4, self.ex)

    def yn(self, d):
        return (self.dp, ((self.y + d + 4) % 4) * 8 + self.k * 2 + self.c)

    def zn(self, d):
        z = (self.z + d + 8) % 8
        return ((z // 4) * 4 + self.x, self.y * 8 + (z % 4) * 2 + self.c)

    def peer(self):
        return (self.dp, self.ex + 1 - 2 * self.c)

    def plane(self, q):
        return (self.dp, q * 2 + self.c)


class Links:
    def __init__(self, send_sem, recv_sem):
        self.send_sem, self.recv_sem, self.count = send_sem, recv_sem, 0
        self.sent = []

    def slot(self):
        self.count += 1
        return self.count - 1

    def start(self, slot, src, dst, dev):
        copy = pltpu.make_async_remote_copy(
            src_ref=src, dst_ref=dst, send_sem=self.send_sem.at[slot], recv_sem=self.recv_sem.at[slot],
            device_id=dev, device_id_type=MESH)
        copy.start()
        self.sent.append(copy)

    def wait(self, slot, dst, dev):
        pltpu.make_async_remote_copy(
            src_ref=dst, dst_ref=dst, send_sem=self.send_sem.at[slot], recv_sem=self.recv_sem.at[slot],
            device_id=dev, device_id_type=MESH).wait_recv()

    def drain(self):
        for copy in self.sent:
            copy.wait_send()
        self.sent = []


class Gather:
    def __init__(self, links, unit, nb, i, own=None):
        self.links, self.unit, self.nb, self.i = links, unit, nb, i
        self.own = own or (lambda h: unit(i, h))
        self.s = [links.slot() for _ in range(6)]

    def send(self):
        l, u, i, s, nb = self.links, self.unit, self.i, self.s, self.nb
        l.start(s[0], self.own(0), u(i, 0), nb(1))
        l.start(s[1], self.own(1), u(i, 1), nb(-1))
        l.start(s[2], self.own(1), u(i, 1), nb(1))
        l.start(s[3], self.own(0), u(i, 0), nb(-1))

    def forward(self):
        l, u, s, nb = self.links, self.unit, self.s, self.nb
        left, right = (self.i + 3) % 4, (self.i + 1) % 4
        l.wait(s[0], u(left, 0), nb(-1))
        l.start(s[4], u(left, 0), u(left, 0), nb(1))
        l.wait(s[1], u(right, 1), nb(1))
        l.start(s[5], u(right, 1), u(right, 1), nb(-1))

    def near(self):
        l, u, s, nb = self.links, self.unit, self.s, self.nb
        left, right = (self.i + 3) % 4, (self.i + 1) % 4
        l.wait(s[2], u(left, 1), nb(-1))
        l.wait(s[3], u(right, 0), nb(1))

    def far(self):
        l, u, s, nb = self.links, self.unit, self.s, self.nb
        opp = (self.i + 2) % 4
        l.wait(s[4], u(opp, 0), nb(-1))
        l.wait(s[5], u(opp, 1), nb(1))


def greet(devices):
    barrier = pltpu.get_barrier_semaphore()
    for dev in devices:
        pl.semaphore_signal(barrier, inc=1, device_id=dev, device_id_type=MESH)
    pl.semaphore_wait(barrier, len(devices))


def k1_body(tokens, wt, gate, up, down, sgate, sup,
            act_a, act_b, act_c, sact, down_peer,
            X, T, W, SW, WT, acc, send_sem, recv_sem, local_sem, wt_send, wt_recv):
    me = Place()
    x, y, k = me.x, me.y, me.k
    q_me = y * 4 + k
    qx = pl.ds(pl.multiple_of(QBASE + QW * x, 128), QW)
    c1 = pl.ds(C1[0], C1[1])
    c2 = pl.ds(C2[0], C2[1])
    both = pl.ds(0, QBASE)

    locals_ = [
        pltpu.make_async_copy(tokens.at[:, both], X.at[y, k, :, both], local_sem.at[0]),
        pltpu.make_async_copy(tokens.at[:, qx], X.at[y, k, :, qx], local_sem.at[1]),
        pltpu.make_async_copy(gate, W.at[0], local_sem.at[2]),
        pltpu.make_async_copy(up, W.at[2], local_sem.at[3]),
        pltpu.make_async_copy(tokens, T, local_sem.at[4]),
        pltpu.make_async_copy(sgate, SW.at[0], local_sem.at[5]),
        pltpu.make_async_copy(sup, SW.at[1], local_sem.at[6]),
    ]
    for copy in locals_:
        copy.start()

    hops = [me.plane((q_me + d) % 16) for d in range(1, 16)]
    greet(hops + [me.xn(1), me.xn(-1), me.zn(1), me.zn(-1), me.peer()])

    links = Links(send_sem, recv_sem)

    def rows(h):
        return pl.ds(64 * h, 64)

    def two(h):
        return pl.ds(2 * h, 2)

    g3y = Gather(links, lambda u, h: X.at[u, k, rows(h), qx], me.yn, y, lambda h: tokens.at[rows(h), qx])
    g1y = Gather(links, lambda u, h: X.at[u, k, rows(h), c1], me.yn, y, lambda h: tokens.at[rows(h), c1])
    g2z = Gather(links, lambda u, h: X.at[y, u, rows(h), c2], me.zn, k, lambda h: tokens.at[rows(h), c2])
    g3z = Gather(links, lambda u, h: X.at[two(h), u, :, qx], me.zn, k)
    g1z = Gather(links, lambda u, h: X.at[two(h), u, :, c1], me.zn, k)
    g2y = Gather(links, lambda u, h: X.at[u, two(h), :, c2], me.yn, y)

    def qcol(u):
        return pl.ds(pl.multiple_of(QBASE + QW * u, 128), QW)

    g3x = [Gather(links, functools.partial(lambda s, u, h: X.at[two(h), s, :, qcol(u)], (k + d) % 4), me.xn, x)
           for d in range(4)]

    g3y.send()
    g1y.send()
    g2z.send()
    for d in range(1, 16):
        q = (q_me + d) % 16
        pltpu.make_async_remote_copy(
            src_ref=wt.at[q], dst_ref=WT.at[q_me], send_sem=wt_send.at[d], recv_sem=wt_recv.at[d],
            device_id=me.plane(q), device_id_type=MESH).start()
    WT[q_me] = wt[q_me]
    peer = me.peer()
    swaps = []
    for n, (src, dst) in enumerate(((gate, W.at[1]), (up, W.at[3]), (down, down_peer))):
        slot = links.slot()
        swaps.append((slot, dst))
        links.start(slot, src, dst, peer)

    locals_[0].wait()
    locals_[1].wait()
    g3y.forward()
    g3y.near()
    g3y.far()
    g3z.send()
    g3x[0].send()
    g2z.forward()
    g1y.forward()
    acc[...] = jnp.zeros_like(acc)
    g2z.near()
    g2z.far()
    g2y.send()
    g1y.near()
    g1y.far()
    g1z.send()

    def dots(part, read, cols, write):
        lo, width = cols

        def step(n, carry):
            res = jnp.dot(read(lo, width), W[n, lo:lo + width, :], preferred_element_type=F32)
            write(n, res)
            return carry

        lax.fori_loop(0, 4, step, 0)

    def by_column(s, cols):
        def read(lo, width):
            return X[:, s, :, lo:lo + width].reshape(4 * TOK, width)

        def write(n, res):
            acc[n, :, s] += res.reshape(4, TOK, HID)

        dots(0, read, cols, write)

    def by_row(u, cols):
        def read(lo, width):
            return X[u, :, :, lo:lo + width].reshape(4 * TOK, width)

        def write(n, res):
            acc[n, u] += res.reshape(4, TOK, HID)

        dots(0, read, cols, write)

    g3x[0].forward()
    for copy in locals_[2:]:
        copy.wait()
    sg = jnp.dot(T[...], SW[0], preferred_element_type=F32)
    su = jnp.dot(T[...], SW[1], preferred_element_type=F32)
    sact[...] = (sg / (1.0 + jnp.exp(-sg)) * su).astype(BF16)
    g3z.forward()
    g3x[0].near()
    g3z.near()
    g3x[1].send()
    g3x[3].send()
    g3x[0].far()
    g3z.far()
    g3x[2].send()
    for slot, dst in swaps[:2]:
        links.wait(slot, dst, peer)
    by_column(k, C1)
    g3x[1].forward()
    g3x[3].forward()
    by_column(k, (QBASE, D - QBASE))
    by_row(y, C2)
    g1z.forward()
    g2y.forward()
    g3x[2].forward()
    g3x[1].near()
    g3x[1].far()
    by_column((k + 1) % 4, (QBASE, D - QBASE))
    g3x[3].near()
    g3x[3].far()
    by_column((k + 3) % 4, (QBASE, D - QBASE))
    g1z.near()
    by_column((k + 1) % 4, C1)
    by_column((k + 3) % 4, C1)
    g2y.near()
    by_row((y + 1) % 4, C2)
    by_row((y + 3) % 4, C2)
    g3x[2].near()
    g3x[2].far()
    by_column((k + 2) % 4, (QBASE, D - QBASE))
    g1z.far()
    by_column((k + 2) % 4, C1)
    g2y.far()
    by_row((y + 2) % 4, C2)

    for d in range(1, 16):
        q = (q_me + 16 - d) % 16
        pltpu.make_async_remote_copy(
            src_ref=wt.at[q], dst_ref=WT.at[q], send_sem=wt_send.at[d], recv_sem=wt_recv.at[d],
            device_id=me.plane(q), device_id_type=MESH).wait()

    def finish(b, carry):
        yb, kb = b // 4, b % 4
        w = jnp.transpose(WT[b])
        halves = []
        for n in range(2):
            g = acc[n, yb, kb]
            u = acc[2 + n, yb, kb]
            halves.append((g / (1.0 + jnp.exp(-g)) * u * w[:, n:n + 1]).astype(BF16))
        for n in range(2):
            hs = pl.ds(n * HID, HID)
            act_a[yb, kb, :, hs] = halves[n][0:48]
            act_b[yb, kb, :, hs] = halves[n][48:96]
            act_c[kb, yb, :, hs] = halves[n][96:128]
        return carry

    lax.fori_loop(0, 16, finish, 0)
    links.wait(swaps[2][0], swaps[2][1], peer)
    links.drain()


class Reduce:
    def __init__(self, links, part, bufs, nb, i, add, add3):
        self.links, self.part, self.bufs, self.nb, self.i = links, part, bufs, nb, i
        self.add, self.add3 = add, add3
        self.s = [links.slot() for _ in range(6)]

    def t(self, d):
        return (self.i + d + 4) % 4

    def first(self):
        l, p, b, s = self.links, self.part, self.bufs, self.s
        l.start(s[0], p(self.t(2), 0), b(0), self.nb(1))
        l.start(s[1], p(self.t(2), 1), b(1), self.nb(-1))

    def second_right(self):
        self.links.start(self.s[2], self.part(self.t(1), 1), self.bufs(2), self.nb(1))

    def second_left(self):
        self.links.start(self.s[3], self.part(self.t(-1), 0), self.bufs(3), self.nb(-1))

    def third(self):
        l, p, b, s = self.links, self.part, self.bufs, self.s
        l.wait(s[0], b(0), self.nb(-1))
        self.add(p(self.t(1), 0), b(0))
        l.start(s[4], p(self.t(1), 0), b(4), self.nb(1))
        l.wait(s[1], b(1), self.nb(1))
        self.add(p(self.t(-1), 1), b(1))
        l.start(s[5], p(self.t(-1), 1), b(5), self.nb(-1))

    def last(self):
        l, p, b, s = self.links, self.part, self.bufs, self.s
        l.wait(s[3], b(3), self.nb(1))
        l.wait(s[4], b(4), self.nb(-1))
        self.add3(p(self.i, 0), b(3), b(4))
        l.wait(s[2], b(2), self.nb(-1))
        l.wait(s[5], b(5), self.nb(1))
        self.add3(p(self.i, 1), b(2), b(5))


def k2_body(act_a, act_b, act_c, sact, down, down_peer, sdown, out,
            PA, PB, PC, A1, A2, A3, A4, B1, B2, B3, B4, CC1, CC2, CC3, CC4,
            DW, SD, F, E, G, send_sem, recv_sem):
    me = Place()
    x, y, k = me.x, me.y, me.k
    greet([me.xn(1), me.xn(-1), me.yn(1), me.yn(-1), me.zn(1), me.zn(-1), me.zn(4)])
    links = Links(send_sem, recv_sem)

    def add2d(dst, a):
        dst[...] = (dst[...].astype(F32) + a[...].astype(F32)).astype(BF16)

    def add3_2d(dst, a, b):
        dst[...] = (dst[...].astype(F32) + a[...].astype(F32) + b[...].astype(F32)).astype(BF16)

    def add3d(dst, a):
        lax.fori_loop(0, dst.shape[0], lambda n, t: (add2d(dst.at[n], a.at[n]), t)[1], 0)

    def add3_3d(dst, a, b):
        lax.fori_loop(0, dst.shape[0], lambda n, t: (add3_2d(dst.at[n], a.at[n], b.at[n]), t)[1], 0)

    def add4d(dst, a):
        w = dst.shape[1]
        lax.fori_loop(0, dst.shape[0] * w, lambda n, t: (add2d(dst.at[n // w, n % w], a.at[n // w, n % w]), t)[1], 0)

    def add3_4d(dst, a, b):
        w = dst.shape[1]
        lax.fori_loop(
            0, dst.shape[0] * w,
            lambda n, t: (add3_2d(dst.at[n // w, n % w], a.at[n // w, n % w], b.at[n // w, n % w]), t)[1], 0)

    def permute(dst, src, base):
        for xx in range(4):
            dst[xx, base:base + HID] = jnp.concatenate(
                [src[:, 448 * xx:448 * xx + 448], src[:, 1792 + 448 * xx:1792 + 448 * xx + 448]], axis=1)

    permute(DW, down, 0)
    permute(DW, down_peer, HID)
    permute(SD, sdown, 0)

    NS = ((0, 256), (256, 256), (512, 256), (768, 128))

    def shared(xx, off, rows):
        return jnp.dot(sact[off:off + rows, :], SD[xx], preferred_element_type=F32)

    def down_a(t):
        def body(m, carry):
            lhs = act_a[pl.ds(2 * m, 2)].reshape(8 * 48, 512)
            for lo, w in NS:
                r = jnp.dot(lhs, DW[t, :, lo:lo + w], preferred_element_type=F32)
                PA[t, pl.ds(2 * m, 2), :, :, lo:lo + w] = r.astype(BF16).reshape(2, 4, 48, w)
            return carry
        lax.fori_loop(0, 2, body, 0)
        PA[t, y, k] = (PA[t, y, k].astype(F32) + shared(t, 0, 48)).astype(BF16)

    def down_b(t):
        def body(xx, carry):
            lhs = act_b[t].reshape(4 * 48, 512)
            for lo, w in NS:
                r = jnp.dot(lhs, DW[xx, :, lo:lo + w], preferred_element_type=F32)
                PB[t, :, xx, :, lo:lo + w] = r.astype(BF16).reshape(4, 48, w)
            return carry
        lax.fori_loop(0, 4, body, 0)

    def down_c(t):
        def body(xx, carry):
            lhs = act_c[t].reshape(4 * 32, 512)
            for lo, w in NS:
                r = jnp.dot(lhs, DW[xx, :, lo:lo + w], preferred_element_type=F32)
                PC[t, xx, :, :, lo:lo + w] = r.astype(BF16).reshape(4, 32, w)
            return carry
        lax.fori_loop(0, 4, body, 0)

    def two(h):
        return pl.ds(2 * h, 2)

    def part_rows(p, h):
        return pl.ds(0, SPLIT[p]) if h == 0 else pl.ds(SPLIT[p], ROWS[p] - SPLIT[p])

    def last_bufs(p, pair):
        return lambda n: pair[0].at[n // 2] if n in (0, 3, 4) else pair[1].at[n // 2]

    ra = Reduce(links, lambda t, h: PA.at[t, two(h)], lambda n: A1.at[n], me.xn, x, add4d, add3_4d)
    rb = Reduce(links, lambda t, h: PB.at[t, two(h)], lambda n: B1.at[n], me.yn, y, add4d, add3_4d)
    rc = Reduce(links, lambda t, h: PC.at[t, two(h)], lambda n: CC1.at[n], me.zn, k, add4d, add3_4d)
    down_a((x + 2) % 4)
    ra.first()
    down_b((y + 2) % 4)
    rb.first()
    down_c((k + 2) % 4)
    rc.first()
    down_a((x + 1) % 4)
    ra.second_right()
    down_a((x + 3) % 4)
    ra.second_left()
    down_b((y + 1) % 4)
    rb.second_right()
    down_b((y + 3) % 4)
    rb.second_left()
    down_c((k + 1) % 4)
    rc.second_right()
    down_c((k + 3) % 4)
    rc.second_left()
    ra.third()
    rb.third()
    rc.third()
    down_a(x)
    down_b(y)
    down_c(k)

    def own_shared(xx, carry):
        PB[y, k, xx] = (PB[y, k, xx].astype(F32) + shared(xx, 48, 48)).astype(BF16)
        PC[k, xx, y] = (PC[k, xx, y].astype(F32) + shared(xx, 96, 32)).astype(BF16)
        return carry

    lax.fori_loop(0, 4, own_shared, 0)

    def run(stages):
        for st in stages:
            st.first()
        for st in stages:
            st.second_right()
            st.second_left()
        for st in stages:
            st.third()

    ra.last()
    rb.last()
    rc.last()
    sa = Reduce(links, lambda t, h: PA.at[x, t, two(h)], lambda n: A2.at[n], me.yn, y, add3d, add3_3d)
    sb = Reduce(links, lambda t, h: PB.at[y, t, two(h)], lambda n: B2.at[n], me.zn, k, add3d, add3_3d)
    sc = Reduce(links, lambda t, h: PC.at[k, t, two(h)], lambda n: CC2.at[n], me.xn, x, add3d, add3_3d)
    run((sa, sb, sc))
    sa.last()
    sb.last()
    sc.last()
    ta = Reduce(links, lambda t, h: PA.at[x, y, t, part_rows(0, h)], last_bufs(0, (A3, A4)), me.zn, k, add2d, add3_2d)
    tb = Reduce(links, lambda t, h: PB.at[y, k, t, part_rows(1, h)], last_bufs(1, (B3, B4)), me.xn, x, add2d, add3_2d)
    tc = Reduce(links, lambda t, h: PC.at[k, x, t, part_rows(2, h)], last_bufs(2, (CC3, CC4)), me.yn, y, add2d, add3_2d)
    run((ta, tb, tc))
    ta.last()
    tb.last()
    tc.last()
    F[0:48] = PA[x, y, k]
    F[48:96] = PB[y, k, x]
    F[96:128] = PC[k, x, y]
    lo = F[:, 0:448].astype(F32)
    hi = F[:, 448:896].astype(F32)
    low = me.zh == 0
    E[...] = jnp.where(low, hi, lo).astype(BF16)
    slot = links.slot()
    links.start(slot, E, G, me.zn(4))
    links.wait(slot, G, me.zn(4))
    out[...] = (jnp.where(low, lo, hi) + G[...].astype(F32)).astype(BF16)
    links.drain()


VM = pl.BlockSpec(memory_space=pltpu.VMEM)
ANY = pl.BlockSpec(memory_space=pl.ANY)


def local(tokens, expert_ids, route_weight, pair_swap, expert_gate, expert_up, expert_down,
          shared_gate, shared_up, shared_down):
    core = lax.axis_index("expert") % 2
    swap = pair_swap.reshape(8, 2)
    swap = jnp.where(core == 1, swap[:, ::-1], swap)
    swap = jnp.concatenate([swap, swap], axis=0)
    column = jnp.arange(32, dtype=jnp.int32).reshape(16, 2)
    column = jnp.where(core == 1, column[:, ::-1], column)
    stored = jnp.where(swap == 1, (column + 16) % 32, column)
    stored = jnp.pad(stored, ((0, 0), (0, 6)), constant_values=-1)
    mix = routed_scale * (route_weight / jnp.sum(route_weight, axis=1, keepdims=True))
    wt = jnp.sum(
        jnp.where(expert_ids.T[:, None, None, :] == stored[None, :, :, None], mix.T[:, None, None, :], 0.0), axis=0)

    shape = jax.ShapeDtypeStruct
    scratch = pltpu.VMEM
    dma = pltpu.SemaphoreType.DMA
    act_a, act_b, act_c, sact, down_peer = pl.pallas_call(
        k1_body,
        name="gather_gate_up",
        out_shape=(shape((4, 4, 48, 512), BF16), shape((4, 4, 48, 512), BF16), shape((4, 4, 32, 512), BF16),
                   shape((TOK, HID), BF16), shape((HID, D), BF16)),
        in_specs=[ANY, VM, ANY, ANY, ANY, ANY, ANY],
        out_specs=(VM, VM, VM, VM, ANY),
        scratch_shapes=[
            scratch((4, 4, TOK, D), BF16),
            scratch((TOK, D), BF16),
            scratch((4, D, HID), BF16),
            scratch((2, D, HID), BF16),
            scratch((16, 8, TOK), F32),
            scratch((4, 4, 4, TOK, HID), F32),
            dma((64,)), dma((64,)), dma((8,)), dma((16,)), dma((16,)),
        ],
        compiler_params=pltpu.CompilerParams(collective_id=0, has_side_effects=True, vmem_limit_bytes=58 << 20),
    )(tokens, wt, expert_gate[0], expert_up[0], expert_down[0], shared_gate, shared_up)

    return pl.pallas_call(
        k2_body,
        name="down_reduce",
        out_shape=shape((TOK, 448), BF16),
        in_specs=[VM] * 7,
        out_specs=VM,
        scratch_shapes=[
            scratch((4, 4, 4, 48, XC), BF16), scratch((4, 4, 4, 48, XC), BF16), scratch((4, 4, 4, 32, XC), BF16),
            scratch((6, 2, 4, 48, XC), BF16), scratch((6, 2, 48, XC), BF16),
            scratch((3, 32, XC), BF16), scratch((3, 16, XC), BF16),
            scratch((6, 2, 4, 48, XC), BF16), scratch((6, 2, 48, XC), BF16),
            scratch((3, 32, XC), BF16), scratch((3, 16, XC), BF16),
            scratch((6, 2, 4, 32, XC), BF16), scratch((6, 2, 32, XC), BF16),
            scratch((3, 16, XC), BF16), scratch((3, 16, XC), BF16),
            scratch((4, 512, XC), BF16), scratch((4, HID, XC), BF16),
            scratch((TOK, XC), BF16), scratch((TOK, 448), BF16), scratch((TOK, 448), BF16),
            dma((64,)), dma((64,)),
        ],
        compiler_params=pltpu.CompilerParams(collective_id=1, has_side_effects=True, vmem_limit_bytes=58 << 20),
    )(act_a, act_b, act_c, sact, expert_down[0], down_peer, shared_down)


def solution(mesh):
    in_specs = (
        P("expert", None),
        P("expert", None),
        P("expert", None),
        P(),
        P("expert", None, "dp"),
        P("expert", None, "dp"),
        P("expert", "dp", None),
        P(None, "dp"),
        P(None, "dp"),
        P("dp", None),
    )
    return jax.shard_map(local, mesh=mesh, in_specs=in_specs, out_specs=P("expert", "dp"), check_vma=False)
```

```python
import functools

import jax
import jax.numpy as jnp
from jax import lax
from jax.experimental import pallas as pl
from jax.experimental.pallas import tpu as pltpu
from jax.sharding import PartitionSpec as P

MESH = pl.DeviceIdType.MESH
F32 = jnp.float32
BF16 = jnp.bfloat16
routed_scale = 2.5
D = 3584
TOK = 128
HID = 256
C1 = (0, 896)
C2 = (896, 1152)
QBASE, QW = 2048, 384
ROWS = (48, 48, 32)
OFFS = (0, 48, 96)
XC = 896
SPLIT = (32, 32, 16)


class Place:
    def __init__(self):
        self.dp = lax.axis_index("dp")
        self.ex = lax.axis_index("expert")
        self.x = self.dp % 4
        self.zh = self.dp // 4
        self.y = self.ex // 8
        self.k = (self.ex // 2) % 4
        self.c = self.ex % 2
        self.z = self.zh * 4 + self.k

    def xn(self, d):
        return (self.zh * 4 + (self.x + d + 4) % 4, self.ex)

    def yn(self, d):
        return (self.dp, ((self.y + d + 4) % 4) * 8 + self.k * 2 + self.c)

    def zn(self, d):
        z = (self.z + d + 8) % 8
        return ((z // 4) * 4 + self.x, self.y * 8 + (z % 4) * 2 + self.c)

    def peer(self):
        return (self.dp, self.ex + 1 - 2 * self.c)

    def plane(self, q):
        return (self.dp, q * 2 + self.c)


class Links:
    def __init__(self, send_sem, recv_sem):
        self.send_sem, self.recv_sem, self.count = send_sem, recv_sem, 0
        self.sent = []

    def slot(self):
        self.count += 1
        return self.count - 1

    def start(self, slot, src, dst, dev):
        copy = pltpu.make_async_remote_copy(
            src_ref=src, dst_ref=dst, send_sem=self.send_sem.at[slot], recv_sem=self.recv_sem.at[slot],
            device_id=dev, device_id_type=MESH)
        copy.start()
        self.sent.append(copy)

    def wait(self, slot, dst, dev):
        pltpu.make_async_remote_copy(
            src_ref=dst, dst_ref=dst, send_sem=self.send_sem.at[slot], recv_sem=self.recv_sem.at[slot],
            device_id=dev, device_id_type=MESH).wait_recv()

    def drain(self):
        for copy in self.sent:
            copy.wait_send()
        self.sent = []


class Gather:
    def __init__(self, links, unit, nb, i, own=None):
        self.links, self.unit, self.nb, self.i = links, unit, nb, i
        self.own = own or (lambda h: unit(i, h))
        self.s = [links.slot() for _ in range(6)]

    def send(self):
        l, u, i, s, nb = self.links, self.unit, self.i, self.s, self.nb
        l.start(s[0], self.own(0), u(i, 0), nb(1))
        l.start(s[1], self.own(1), u(i, 1), nb(-1))
        l.start(s[2], self.own(1), u(i, 1), nb(1))
        l.start(s[3], self.own(0), u(i, 0), nb(-1))

    def forward(self):
        l, u, s, nb = self.links, self.unit, self.s, self.nb
        left, right = (self.i + 3) % 4, (self.i + 1) % 4
        l.wait(s[0], u(left, 0), nb(-1))
        l.start(s[4], u(left, 0), u(left, 0), nb(1))
        l.wait(s[1], u(right, 1), nb(1))
        l.start(s[5], u(right, 1), u(right, 1), nb(-1))

    def near(self):
        l, u, s, nb = self.links, self.unit, self.s, self.nb
        left, right = (self.i + 3) % 4, (self.i + 1) % 4
        l.wait(s[2], u(left, 1), nb(-1))
        l.wait(s[3], u(right, 0), nb(1))

    def far(self):
        l, u, s, nb = self.links, self.unit, self.s, self.nb
        opp = (self.i + 2) % 4
        l.wait(s[4], u(opp, 0), nb(-1))
        l.wait(s[5], u(opp, 1), nb(1))


def greet(devices):
    barrier = pltpu.get_barrier_semaphore()
    for dev in devices:
        pl.semaphore_signal(barrier, inc=1, device_id=dev, device_id_type=MESH)
    pl.semaphore_wait(barrier, len(devices))


def gather_phase(me, links, tokens, ids, rw, swap, gate, up, down, sgate, sup, sdown, act, DW, S, sem,
                 X, W, SW, RAW, acc, WT, wt, T):
    x, y, k = me.x, me.y, me.k
    q_me = y * 4 + k
    c1 = pl.ds(C1[0], C1[1])
    c2 = pl.ds(C2[0], C2[1])
    both = pl.ds(0, QBASE)
    act_a, act_b, act_c = act
    local_sem, wt_send, wt_recv = sem

    def qcol(u):
        return pl.ds(pl.multiple_of(QBASE + QW * u, 128), QW)

    qx = qcol(x)

    def load(src, dst, n):
        copy = pltpu.make_async_copy(src, dst, local_sem.at[n])
        copy.start()
        return copy

    own0 = load(tokens.at[:, both], X.at[y, k, :, both], 0)
    own1 = load(tokens.at[:, qx], X.at[y, k, :, qx], 1)
    w_gate = load(gate, W.at[0], 2)
    w_up = load(up, W.at[2], 3)
    w_down = load(down, RAW, 4)
    w_sg = load(sgate, SW, 5)
    w_tok = load(tokens, T, 6)

    hops = [me.plane((q_me + d) % 16) for d in range(1, 16)]
    greet(hops + [me.xn(1), me.xn(-1), me.yn(1), me.yn(-1), me.zn(1), me.zn(-1), me.zn(4), me.peer()])

    def rows(h):
        return pl.ds(64 * h, 64)

    def two(h):
        return pl.ds(2 * h, 2)

    def row(d):
        return (y + d) % 4

    def col(d):
        return (k + d) % 4

    part = functools.partial
    g3y = Gather(links, lambda u, h: X.at[u, k, rows(h), qx], me.yn, y, lambda h: tokens.at[rows(h), qx])
    g1y = Gather(links, lambda u, h: X.at[u, k, rows(h), c1], me.yn, y, lambda h: tokens.at[rows(h), c1])
    g2z = Gather(links, lambda u, h: X.at[y, u, rows(h), c2], me.zn, k, lambda h: tokens.at[rows(h), c2])
    g3z = [Gather(links, part(lambda s, u, h: X.at[s, u, rows(h), qx], row(d)), me.zn, k,
                  (lambda h: tokens.at[rows(h), qx]) if d == 0 else None) for d in range(4)]
    g1z = [Gather(links, part(lambda s, u, h: X.at[s, u, rows(h), c1], row(d)), me.zn, k,
                  (lambda h: tokens.at[rows(h), c1]) if d == 0 else None) for d in range(4)]
    g2y = [Gather(links, part(lambda s, u, h: X.at[u, s, rows(h), c2], col(d)), me.yn, y,
                  (lambda h: tokens.at[rows(h), c2]) if d == 0 else None) for d in range(4)]
    g3x = [Gather(links, part(lambda s, u, h: X.at[s, two(h), :, qcol(u)], row(d)), me.xn, x) for d in range(4)]

    def done(g):
        g.near()
        g.far()

    def dots(read, write, cols):
        lo, width = cols

        def step(n, carry):
            write(n, jnp.dot(read(lo, width), W[n, lo:lo + width, :], preferred_element_type=F32))
            return carry

        lax.fori_loop(0, 4, step, 0)

    def by_column(s, cols):
        def write(n, res):
            acc[n, :, s] += res.reshape(4, TOK, HID)

        dots(lambda lo, width: X[:, s, :, lo:lo + width].reshape(4 * TOK, width), write, cols)

    def by_row(u, cols):
        def write(n, res):
            acc[n, u] += res.reshape(4, TOK, HID)

        dots(lambda lo, width: X[u, :, :, lo:lo + width].reshape(4 * TOK, width), write, cols)

    QC = (QBASE, D - QBASE)

    g3z[0].send()
    g3y.send()
    peer = me.peer()
    swap_gate, swap_up, swap_down = links.slot(), links.slot(), links.slot()
    links.start(swap_gate, gate, W.at[1], peer)
    links.start(swap_up, up, W.at[3], peer)
    weight = rw[...]
    mix = routed_scale * (weight / jnp.sum(weight, axis=0, keepdims=True))
    chosen = ids[...]
    lane_row = lax.broadcasted_iota(jnp.int32, (8, TOK), 0)
    for q in range(16):
        tile = jnp.zeros((8, TOK), F32)
        for r, column in enumerate((2 * q + me.c, 2 * q + 1 - me.c)):
            stored = (column + 16 * swap[column % 16]) % 32
            picked = jnp.sum(jnp.where(chosen == stored, mix, 0.0), axis=0, keepdims=True)
            tile = jnp.where(lane_row == r, picked, tile)
        wt[q] = tile
    own0.wait()
    own1.wait()
    g3z[0].forward()
    g3y.forward()
    g1y.send()
    g3y.near()
    g3z[1].send()
    g3z[3].send()
    done(g3z[0])
    g3x[0].send()
    g3y.far()
    g3z[2].send()
    g2y[0].send()
    for d in range(1, 16):
        q = (q_me + d) % 16
        pltpu.make_async_remote_copy(
            src_ref=wt.at[q], dst_ref=WT.at[q_me], send_sem=wt_send.at[d], recv_sem=wt_recv.at[d],
            device_id=me.plane(q), device_id_type=MESH).start()
    WT[q_me] = wt[q_me]
    g3z[1].forward()
    g3z[3].forward()
    g2z.send()
    g3z[2].forward()
    g1z[0].send()
    w_down.wait()
    for xx in range(4):
        DW[xx, 0:HID] = jnp.concatenate(
            [RAW[:, 448 * xx:448 * xx + 448], RAW[:, 1792 + 448 * xx:1792 + 448 * xx + 448]], axis=1)
    links.start(swap_down, DW.at[:, pl.ds(0, HID)], DW.at[:, pl.ds(HID, HID)], peer)
    w_sdown = load(sdown, RAW, 4)
    g1y.forward()
    g3x[0].forward()
    done(g3z[1])
    g3x[1].send()
    done(g3z[3])
    g3x[3].send()
    done(g3z[2])
    g3x[2].send()
    g2z.forward()
    acc[...] = jnp.zeros_like(acc)
    g1y.near()
    g1z[1].send()
    g1z[3].send()
    g1y.far()
    g1z[2].send()
    w_tok.wait()
    w_sg.wait()
    sg = jnp.dot(T[...], SW[...], preferred_element_type=F32)
    w_su = load(sup, SW, 5)
    silu = sg / (1.0 + jnp.exp(-sg))
    g2z.near()
    g2y[1].send()
    g2y[3].send()
    g2y[0].forward()
    g1z[0].forward()
    g2z.far()
    g2y[2].send()
    w_su.wait()
    sact = (silu * jnp.dot(T[...], SW[...], preferred_element_type=F32)).astype(BF16)
    w_gate.wait()
    w_up.wait()
    links.wait(swap_gate, W.at[1], peer)
    links.wait(swap_up, W.at[3], peer)
    done(g3x[0])
    by_row(y, QC)
    g3x[1].forward()
    done(g1z[0])
    by_row(y, C1)
    done(g2y[0])
    g2y[1].forward()
    g1z[1].forward()
    by_column(k, C2)
    w_sdown.wait()
    for xx in range(4):
        S[xx] = jnp.concatenate(
            [jnp.dot(sact, RAW[:, base + 448 * xx:base + 448 * xx + 448], preferred_element_type=F32)
             for base in (0, 1792)], axis=1).astype(BF16)
    g2y[3].forward()
    g1z[3].forward()
    g3x[3].forward()
    done(g2y[1])
    by_column(col(1), C2)
    done(g3x[1])
    by_row(row(1), QC)
    done(g1z[1])
    by_row(row(1), C1)
    g2y[2].forward()
    g1z[2].forward()
    g3x[2].forward()
    done(g2y[3])
    by_column(col(3), C2)
    done(g3x[3])
    by_row(row(3), QC)
    done(g1z[3])
    by_row(row(3), C1)
    for d in range(1, 16):
        q = (q_me + 16 - d) % 16
        pltpu.make_async_remote_copy(
            src_ref=wt.at[q], dst_ref=WT.at[q], send_sem=wt_send.at[d], recv_sem=wt_recv.at[d],
            device_id=me.plane(q), device_id_type=MESH).wait()

    def finish(yb):
        def body(kb, carry):
            w = jnp.transpose(WT[yb * 4 + kb])
            for n in range(2):
                g = acc[n, yb, kb]
                u = acc[2 + n, yb, kb]
                v = (g / (1.0 + jnp.exp(-g)) * u * w[:, n:n + 1]).astype(BF16)
                hs = pl.ds(n * HID, HID)
                act_a[yb, kb, :, hs] = v[0:48]
                act_b[yb, kb, :, hs] = v[48:96]
                act_c[kb, yb, :, hs] = v[96:128]
            return carry

        lax.fori_loop(0, 4, body, 0)

    done(g2y[2])
    by_column(col(2), C2)
    finish(y)
    finish(row(1))
    finish(row(3))
    done(g1z[2])
    by_row(row(2), C1)
    done(g3x[2])
    by_row(row(2), QC)
    finish(row(2))
    links.wait(swap_down, DW.at[:, pl.ds(HID, HID)], peer)
    links.drain()


class Reduce:
    def __init__(self, links, part, bufs, nb, i, add, add3):
        self.links, self.part, self.bufs, self.nb, self.i = links, part, bufs, nb, i
        self.add, self.add3 = add, add3
        self.s = [links.slot() for _ in range(6)]

    def t(self, d):
        return (self.i + d + 4) % 4

    def first(self):
        l, p, b, s = self.links, self.part, self.bufs, self.s
        l.start(s[0], p(self.t(2), 0), b(0), self.nb(1))
        l.start(s[1], p(self.t(2), 1), b(1), self.nb(-1))

    def second_right(self):
        self.links.start(self.s[2], self.part(self.t(1), 1), self.bufs(2), self.nb(1))

    def second_left(self):
        self.links.start(self.s[3], self.part(self.t(-1), 0), self.bufs(3), self.nb(-1))

    def third(self):
        l, p, b, s = self.links, self.part, self.bufs, self.s
        l.wait(s[0], b(0), self.nb(-1))
        self.add(p(self.t(1), 0), b(0))
        l.start(s[4], p(self.t(1), 0), b(4), self.nb(1))
        l.wait(s[1], b(1), self.nb(1))
        self.add(p(self.t(-1), 1), b(1))
        l.start(s[5], p(self.t(-1), 1), b(5), self.nb(-1))

    def last(self):
        l, p, b, s = self.links, self.part, self.bufs, self.s
        l.wait(s[3], b(3), self.nb(1))
        l.wait(s[4], b(4), self.nb(-1))
        self.add3(p(self.i, 0), b(3), b(4))
        l.wait(s[2], b(2), self.nb(-1))
        l.wait(s[5], b(5), self.nb(1))
        self.add3(p(self.i, 1), b(2), b(5))


def reduce_phase(me, links, act, DW, S, bufs, F, E, G, out, PA, PB, PC):
    x, y, k = me.x, me.y, me.k
    act_a, act_b, act_c = act
    (A1, A2, A3, A4), (B1, B2, B3, B4), (CC1, CC2, CC3, CC4) = bufs

    def add2d(dst, a):
        dst[...] = (dst[...].astype(F32) + a[...].astype(F32)).astype(BF16)

    def add3_2d(dst, a, b):
        dst[...] = (dst[...].astype(F32) + a[...].astype(F32) + b[...].astype(F32)).astype(BF16)

    def add3d(dst, a):
        lax.fori_loop(0, dst.shape[0], lambda n, t: (add2d(dst.at[n], a.at[n]), t)[1], 0)

    def add3_3d(dst, a, b):
        lax.fori_loop(0, dst.shape[0], lambda n, t: (add3_2d(dst.at[n], a.at[n], b.at[n]), t)[1], 0)

    def add4d(dst, a):
        w = dst.shape[1]
        lax.fori_loop(0, dst.shape[0] * w, lambda n, t: (add2d(dst.at[n // w, n % w], a.at[n // w, n % w]), t)[1], 0)

    def add3_4d(dst, a, b):
        w = dst.shape[1]
        lax.fori_loop(
            0, dst.shape[0] * w,
            lambda n, t: (add3_2d(dst.at[n // w, n % w], a.at[n // w, n % w], b.at[n // w, n % w]), t)[1], 0)

    NS = ((0, 256), (256, 256), (512, 256), (768, 128))

    def shared(xx, off, rows):
        return S[xx, off:off + rows, :].astype(F32)

    def down_a(t):
        def body(m, carry):
            lhs = act_a[pl.ds(2 * m, 2)].reshape(8 * 48, 512)
            for lo, w in NS:
                r = jnp.dot(lhs, DW[t, :, lo:lo + w], preferred_element_type=F32)
                PA[t, pl.ds(2 * m, 2), :, :, lo:lo + w] = r.astype(BF16).reshape(2, 4, 48, w)
            return carry
        lax.fori_loop(0, 2, body, 0)
        PA[t, y, k] = (PA[t, y, k].astype(F32) + shared(t, 0, 48)).astype(BF16)

    def down_b(t):
        def body(xx, carry):
            lhs = act_b[t].reshape(4 * 48, 512)
            for lo, w in NS:
                r = jnp.dot(lhs, DW[xx, :, lo:lo + w], preferred_element_type=F32)
                PB[t, :, xx, :, lo:lo + w] = r.astype(BF16).reshape(4, 48, w)
            return carry
        lax.fori_loop(0, 4, body, 0)

    def down_c(t):
        def body(xx, carry):
            lhs = act_c[t].reshape(4 * 32, 512)
            for lo, w in NS:
                r = jnp.dot(lhs, DW[xx, :, lo:lo + w], preferred_element_type=F32)
                PC[t, xx, :, :, lo:lo + w] = r.astype(BF16).reshape(4, 32, w)
            return carry
        lax.fori_loop(0, 4, body, 0)

    def two(h):
        return pl.ds(2 * h, 2)

    def part_rows(p, h):
        return pl.ds(0, SPLIT[p]) if h == 0 else pl.ds(SPLIT[p], ROWS[p] - SPLIT[p])

    def last_bufs(p, pair):
        return lambda n: pair[0].at[n // 2] if n in (0, 3, 4) else pair[1].at[n // 2]

    ra = Reduce(links, lambda t, h: PA.at[t, two(h)], lambda n: A1.at[n], me.xn, x, add4d, add3_4d)
    rb = Reduce(links, lambda t, h: PB.at[t, two(h)], lambda n: B1.at[n], me.yn, y, add4d, add3_4d)
    rc = Reduce(links, lambda t, h: PC.at[t, two(h)], lambda n: CC1.at[n], me.zn, k, add4d, add3_4d)
    down_a((x + 2) % 4)
    ra.first()
    down_b((y + 2) % 4)
    rb.first()
    down_c((k + 2) % 4)
    rc.first()
    down_a((x + 1) % 4)
    ra.second_right()
    down_a((x + 3) % 4)
    ra.second_left()
    down_b((y + 1) % 4)
    rb.second_right()
    down_b((y + 3) % 4)
    rb.second_left()
    down_c((k + 1) % 4)
    rc.second_right()
    down_c((k + 3) % 4)
    rc.second_left()
    ra.third()
    rb.third()
    rc.third()
    down_a(x)
    down_b(y)
    down_c(k)

    def own_shared(xx, carry):
        PB[y, k, xx] = (PB[y, k, xx].astype(F32) + shared(xx, 48, 48)).astype(BF16)
        PC[k, xx, y] = (PC[k, xx, y].astype(F32) + shared(xx, 96, 32)).astype(BF16)
        return carry

    lax.fori_loop(0, 4, own_shared, 0)

    def run(stages):
        for st in stages:
            st.first()
        for st in stages:
            st.second_right()
            st.second_left()
        for st in stages:
            st.third()

    ra.last()
    rb.last()
    rc.last()
    sa = Reduce(links, lambda t, h: PA.at[x, t, two(h)], lambda n: A2.at[n], me.yn, y, add3d, add3_3d)
    sb = Reduce(links, lambda t, h: PB.at[y, t, two(h)], lambda n: B2.at[n], me.zn, k, add3d, add3_3d)
    sc = Reduce(links, lambda t, h: PC.at[k, t, two(h)], lambda n: CC2.at[n], me.xn, x, add3d, add3_3d)
    run((sa, sb, sc))
    sa.last()
    sb.last()
    sc.last()
    ta = Reduce(links, lambda t, h: PA.at[x, y, t, part_rows(0, h)], last_bufs(0, (A3, A4)), me.zn, k, add2d, add3_2d)
    tb = Reduce(links, lambda t, h: PB.at[y, k, t, part_rows(1, h)], last_bufs(1, (B3, B4)), me.xn, x, add2d, add3_2d)
    tc = Reduce(links, lambda t, h: PC.at[k, x, t, part_rows(2, h)], last_bufs(2, (CC3, CC4)), me.yn, y, add2d, add3_2d)
    run((ta, tb, tc))
    ta.last()
    tb.last()
    tc.last()
    F[0:48] = PA[x, y, k]
    F[48:96] = PB[y, k, x]
    F[96:128] = PC[k, x, y]
    lo = F[:, 0:448].astype(F32)
    hi = F[:, 448:896].astype(F32)
    low = me.zh == 0
    E[...] = jnp.where(low, hi, lo).astype(BF16)
    slot = links.slot()
    links.start(slot, E, G, me.zn(4))
    links.wait(slot, G, me.zn(4))
    out[...] = (jnp.where(low, lo, hi) + G[...].astype(F32)).astype(BF16)
    links.drain()


def layer_body(tokens, ids, rw, swap, gate, up, down, sgate, sup, sdown, out,
               act_a, act_b, act_c, DW, S, A1, A2, A3, A4, B1, B2, B3, B4, CC1, CC2, CC3, CC4, F, E, G,
               send_sem, recv_sem, local_sem, wt_send, wt_recv):
    me = Place()
    links = Links(send_sem, recv_sem)
    act = (act_a, act_b, act_c)
    vmem = pltpu.VMEM
    pl.run_scoped(
        functools.partial(gather_phase, me, links, tokens, ids, rw, swap, gate, up, down, sgate, sup, sdown, act, DW, S,
                          (local_sem, wt_send, wt_recv)),
        vmem((4, 4, TOK, D), BF16), vmem((4, D, HID), BF16), vmem((D, HID), BF16), vmem((HID, D), BF16),
        vmem((4, 4, 4, TOK, HID), F32), vmem((16, 8, TOK), F32), vmem((16, 8, TOK), F32), vmem((TOK, D), BF16))
    pl.run_scoped(
        functools.partial(reduce_phase, me, links, act, DW, S,
                          ((A1, A2, A3, A4), (B1, B2, B3, B4), (CC1, CC2, CC3, CC4)), F, E, G, out),
        vmem((4, 4, 4, 48, XC), BF16), vmem((4, 4, 4, 48, XC), BF16), vmem((4, 4, 4, 32, XC), BF16))


VM = pl.BlockSpec(memory_space=pltpu.VMEM)
ANY = pl.BlockSpec(memory_space=pl.ANY)


def local(tokens, expert_ids, route_weight, pair_swap, expert_gate, expert_up, expert_down,
          shared_gate, shared_up, shared_down):
    shape = jax.ShapeDtypeStruct
    scratch = pltpu.VMEM
    dma = pltpu.SemaphoreType.DMA
    return pl.pallas_call(
        layer_body,
        name="expert_layer",
        out_shape=shape((TOK, 448), BF16),
        in_specs=[ANY, VM, VM, pl.BlockSpec(memory_space=pltpu.SMEM), ANY, ANY, ANY, ANY, ANY, ANY],
        out_specs=VM,
        scratch_shapes=[
            scratch((4, 4, 48, 512), BF16), scratch((4, 4, 48, 512), BF16), scratch((4, 4, 32, 512), BF16),
            scratch((4, 512, XC), BF16), scratch((4, TOK, XC), BF16),
            scratch((6, 2, 4, 48, XC), BF16), scratch((6, 2, 48, XC), BF16),
            scratch((3, 32, XC), BF16), scratch((3, 16, XC), BF16),
            scratch((6, 2, 4, 48, XC), BF16), scratch((6, 2, 48, XC), BF16),
            scratch((3, 32, XC), BF16), scratch((3, 16, XC), BF16),
            scratch((6, 2, 4, 32, XC), BF16), scratch((6, 2, 32, XC), BF16),
            scratch((3, 16, XC), BF16), scratch((3, 16, XC), BF16),
            scratch((TOK, XC), BF16), scratch((TOK, 448), BF16), scratch((TOK, 448), BF16),
            dma((192,)), dma((192,)), dma((8,)), dma((16,)), dma((16,)),
        ],
        compiler_params=pltpu.CompilerParams(collective_id=0, has_side_effects=True, vmem_limit_bytes=63 << 20),
    )(tokens, expert_ids.T, route_weight.T, pair_swap, expert_gate[0], expert_up[0], expert_down[0], shared_gate, shared_up, shared_down)


def solution(mesh):
    in_specs = (
        P("expert", None),
        P("expert", None),
        P("expert", None),
        P(),
        P("expert", None, "dp"),
        P("expert", None, "dp"),
        P("expert", "dp", None),
        P(None, "dp"),
        P(None, "dp"),
        P("dp", None),
    )
    return jax.shard_map(local, mesh=mesh, in_specs=in_specs, out_specs=P("expert", "dp"), check_vma=False)
```

```python
import functools

import jax
import jax.numpy as jnp
from jax import lax
from jax.experimental import pallas as pl
from jax.experimental.pallas import tpu as pltpu
from jax.sharding import PartitionSpec as P

MESH = pl.DeviceIdType.MESH
F32 = jnp.float32
BF16 = jnp.bfloat16
routed_scale = 2.5
D = 3584
TOK = 128
HID = 256
C1 = (0, 896)
C2 = (896, 1152)
QBASE, QW = 2048, 384
ROWS = (48, 48, 32)
OFFS = (0, 48, 96)
XC = 896
SPLIT = (32, 32, 16)


class Place:
    def __init__(self):
        self.dp = lax.axis_index("dp")
        self.ex = lax.axis_index("expert")
        self.x = self.dp % 4
        self.zh = self.dp // 4
        self.y = self.ex // 8
        self.k = (self.ex // 2) % 4
        self.c = self.ex % 2
        self.z = self.zh * 4 + self.k

    def xn(self, d):
        return (self.zh * 4 + (self.x + d + 4) % 4, self.ex)

    def yn(self, d):
        return (self.dp, ((self.y + d + 4) % 4) * 8 + self.k * 2 + self.c)

    def zn(self, d):
        z = (self.z + d + 8) % 8
        return ((z // 4) * 4 + self.x, self.y * 8 + (z % 4) * 2 + self.c)

    def peer(self):
        return (self.dp, self.ex + 1 - 2 * self.c)

    def plane(self, q):
        return (self.dp, q * 2 + self.c)


class Links:
    def __init__(self, send_sem, recv_sem):
        self.send_sem, self.recv_sem, self.count = send_sem, recv_sem, 0
        self.sent = []

    def slot(self):
        self.count += 1
        return self.count - 1

    def start(self, slot, src, dst, dev):
        copy = pltpu.make_async_remote_copy(
            src_ref=src, dst_ref=dst, send_sem=self.send_sem.at[slot], recv_sem=self.recv_sem.at[slot],
            device_id=dev, device_id_type=MESH)
        copy.start()
        self.sent.append(copy)

    def wait(self, slot, dst, dev):
        pltpu.make_async_remote_copy(
            src_ref=dst, dst_ref=dst, send_sem=self.send_sem.at[slot], recv_sem=self.recv_sem.at[slot],
            device_id=dev, device_id_type=MESH).wait_recv()

    def drain(self):
        for copy in self.sent:
            copy.wait_send()
        self.sent = []


class Gather:
    def __init__(self, links, unit, nb, i, own=None):
        self.links, self.unit, self.nb, self.i = links, unit, nb, i
        self.own = own or (lambda h: unit(i, h))
        self.s = [links.slot() for _ in range(6)]

    def send(self):
        l, u, i, s, nb = self.links, self.unit, self.i, self.s, self.nb
        l.start(s[0], self.own(0), u(i, 0), nb(1))
        l.start(s[1], self.own(1), u(i, 1), nb(-1))
        l.start(s[2], self.own(1), u(i, 1), nb(1))
        l.start(s[3], self.own(0), u(i, 0), nb(-1))

    def forward(self):
        l, u, s, nb = self.links, self.unit, self.s, self.nb
        left, right = (self.i + 3) % 4, (self.i + 1) % 4
        l.wait(s[0], u(left, 0), nb(-1))
        l.start(s[4], u(left, 0), u(left, 0), nb(1))
        l.wait(s[1], u(right, 1), nb(1))
        l.start(s[5], u(right, 1), u(right, 1), nb(-1))

    def near(self):
        l, u, s, nb = self.links, self.unit, self.s, self.nb
        left, right = (self.i + 3) % 4, (self.i + 1) % 4
        l.wait(s[2], u(left, 1), nb(-1))
        l.wait(s[3], u(right, 0), nb(1))

    def far(self):
        l, u, s, nb = self.links, self.unit, self.s, self.nb
        opp = (self.i + 2) % 4
        l.wait(s[4], u(opp, 0), nb(-1))
        l.wait(s[5], u(opp, 1), nb(1))


def greet(devices):
    barrier = pltpu.get_barrier_semaphore()
    for dev in devices:
        pl.semaphore_signal(barrier, inc=1, device_id=dev, device_id_type=MESH)
    pl.semaphore_wait(barrier, len(devices))


def gather_phase(me, links, tokens, ids, rw, swap, gate, up, down, sgate, sup, sdown, act, DW, S, sem,
                 X, W, SW, RAW, acc, WT, wt, T):
    x, y, k = me.x, me.y, me.k
    q_me = y * 4 + k
    c1 = pl.ds(C1[0], C1[1])
    c2 = pl.ds(C2[0], C2[1])
    both = pl.ds(0, QBASE)
    act_a, act_b, act_c = act
    local_sem, wt_send, wt_recv = sem

    def qcol(u):
        return pl.ds(pl.multiple_of(QBASE + QW * u, 128), QW)

    qx = qcol(x)

    def load(src, dst, n):
        copy = pltpu.make_async_copy(src, dst, local_sem.at[n])
        copy.start()
        return copy

    own0 = load(tokens.at[:, both], X.at[y, k, :, both], 0)
    own1 = load(tokens.at[:, qx], X.at[y, k, :, qx], 1)
    w_gate = load(gate, W.at[0], 2)
    w_up = load(up, W.at[2], 3)
    w_down = load(down, RAW, 4)
    w_sg = load(sgate, SW, 5)
    w_tok = load(tokens, T, 6)

    hops = [me.plane((q_me + d) % 16) for d in range(1, 16)]
    greet(hops + [me.xn(1), me.xn(-1), me.yn(1), me.yn(-1), me.zn(1), me.zn(-1), me.zn(4), me.peer()])

    def rows(h):
        return pl.ds(64 * h, 64)

    def two(h):
        return pl.ds(2 * h, 2)

    def row(d):
        return (y + d) % 4

    def col(d):
        return (k + d) % 4

    part = functools.partial
    g3y = Gather(links, lambda u, h: X.at[u, k, rows(h), qx], me.yn, y, lambda h: tokens.at[rows(h), qx])
    g1y = Gather(links, lambda u, h: X.at[u, k, rows(h), c1], me.yn, y, lambda h: tokens.at[rows(h), c1])
    g2z = Gather(links, lambda u, h: X.at[y, u, rows(h), c2], me.zn, k, lambda h: tokens.at[rows(h), c2])
    g3z = [Gather(links, part(lambda s, u, h: X.at[s, u, rows(h), qx], row(d)), me.zn, k,
                  (lambda h: tokens.at[rows(h), qx]) if d == 0 else None) for d in range(4)]
    g1z = [Gather(links, part(lambda s, u, h: X.at[s, u, rows(h), c1], row(d)), me.zn, k,
                  (lambda h: tokens.at[rows(h), c1]) if d == 0 else None) for d in range(4)]
    g2y = [Gather(links, part(lambda s, u, h: X.at[u, s, rows(h), c2], col(d)), me.yn, y,
                  (lambda h: tokens.at[rows(h), c2]) if d == 0 else None) for d in range(4)]
    g3x = [Gather(links, part(lambda s, u, h: X.at[s, two(h), :, qcol(u)], row(d)), me.xn, x) for d in range(4)]

    def done(g):
        g.near()
        g.far()

    def dots(read, write, cols):
        lo, width = cols

        def step(n, carry):
            write(n, jnp.dot(read(lo, width), W[n, lo:lo + width, :], preferred_element_type=F32))
            return carry

        lax.fori_loop(0, 4, step, 0)

    def by_column(s, cols):
        def write(n, res):
            acc[n, :, s] += res.reshape(4, TOK, HID)

        dots(lambda lo, width: X[:, s, :, lo:lo + width].reshape(4 * TOK, width), write, cols)

    def by_row(u, cols):
        def write(n, res):
            acc[n, u] += res.reshape(4, TOK, HID)

        dots(lambda lo, width: X[u, :, :, lo:lo + width].reshape(4 * TOK, width), write, cols)

    QC = (QBASE, D - QBASE)

    g3z[0].send()
    g3y.send()
    peer = me.peer()
    swap_gate, swap_up, swap_down = links.slot(), links.slot(), links.slot()
    links.start(swap_gate, gate, W.at[1], peer)
    links.start(swap_up, up, W.at[3], peer)
    weight = rw[...]
    mix = routed_scale * (weight / jnp.sum(weight, axis=0, keepdims=True))
    chosen = ids[...]
    lane_row = lax.broadcasted_iota(jnp.int32, (8, TOK), 0)
    for q in range(16):
        tile = jnp.zeros((8, TOK), F32)
        for r, column in enumerate((2 * q + me.c, 2 * q + 1 - me.c)):
            stored = (column + 16 * swap[column % 16]) % 32
            picked = jnp.sum(jnp.where(chosen == stored, mix, 0.0), axis=0, keepdims=True)
            tile = jnp.where(lane_row == r, picked, tile)
        wt[q] = tile
    own0.wait()
    own1.wait()
    g3z[0].forward()
    g3y.forward()
    g1y.send()
    g3y.near()
    g3z[1].send()
    g3z[3].send()
    done(g3z[0])
    g3x[0].send()
    g3y.far()
    g3z[2].send()
    g2y[0].send()
    for d in range(1, 16):
        q = (q_me + d) % 16
        pltpu.make_async_remote_copy(
            src_ref=wt.at[q], dst_ref=WT.at[q_me], send_sem=wt_send.at[d], recv_sem=wt_recv.at[d],
            device_id=me.plane(q), device_id_type=MESH).start()
    WT[q_me] = wt[q_me]
    g3z[1].forward()
    g3z[3].forward()
    g2z.send()
    g3z[2].forward()
    g1z[0].send()
    w_down.wait()
    for xx in range(4):
        DW[xx, 0:HID] = jnp.concatenate(
            [RAW[:, 448 * xx:448 * xx + 448], RAW[:, 1792 + 448 * xx:1792 + 448 * xx + 448]], axis=1)
    links.start(swap_down, DW.at[:, pl.ds(0, HID)], DW.at[:, pl.ds(HID, HID)], peer)
    w_sdown = load(sdown, RAW, 4)
    g1y.forward()
    g3x[0].forward()
    done(g3z[1])
    g3x[1].send()
    g2z.forward()
    acc[...] = jnp.zeros_like(acc)
    g1y.near()
    g1z[1].send()
    g1y.far()
    done(g3z[3])
    done(g3z[2])
    w_tok.wait()
    w_sg.wait()
    sg = jnp.dot(T[...], SW[...], preferred_element_type=F32)
    w_su = load(sup, SW, 5)
    silu = sg / (1.0 + jnp.exp(-sg))
    g2z.near()
    g2y[1].send()
    g2y[0].forward()
    g3x[1].forward()
    g3x[3].send()
    g1z[0].forward()
    g1z[3].send()
    g2z.far()
    w_su.wait()
    sact = (silu * jnp.dot(T[...], SW[...], preferred_element_type=F32)).astype(BF16)
    w_gate.wait()
    w_up.wait()
    links.wait(swap_gate, W.at[1], peer)
    links.wait(swap_up, W.at[3], peer)
    done(g3x[0])
    by_row(y, QC)
    g2y[1].forward()
    g2y[3].send()
    done(g2y[0])
    by_column(k, C2)
    g1z[1].forward()
    g1z[2].send()
    g3x[3].forward()
    g3x[2].send()
    w_sdown.wait()
    for xx in range(4):
        S[xx] = jnp.concatenate(
            [jnp.dot(sact, RAW[:, base + 448 * xx:base + 448 * xx + 448], preferred_element_type=F32)
             for base in (0, 1792)], axis=1).astype(BF16)
    done(g1z[0])
    by_row(y, C1)
    done(g2y[1])
    by_column(col(1), C2)
    g2y[3].forward()
    g2y[2].send()
    done(g3x[1])
    by_row(row(1), QC)
    g1z[3].forward()
    done(g1z[1])
    by_row(row(1), C1)
    g2y[2].forward()
    g3x[2].forward()
    done(g2y[3])
    by_column(col(3), C2)
    g1z[2].forward()
    done(g3x[3])
    by_row(row(3), QC)
    done(g1z[3])
    by_row(row(3), C1)
    for d in range(1, 16):
        q = (q_me + 16 - d) % 16
        pltpu.make_async_remote_copy(
            src_ref=wt.at[q], dst_ref=WT.at[q], send_sem=wt_send.at[d], recv_sem=wt_recv.at[d],
            device_id=me.plane(q), device_id_type=MESH).wait()

    def finish(yb):
        def body(kb, carry):
            w = jnp.transpose(WT[yb * 4 + kb])
            for n in range(2):
                g = acc[n, yb, kb]
                u = acc[2 + n, yb, kb]
                v = (g / (1.0 + jnp.exp(-g)) * u * w[:, n:n + 1]).astype(BF16)
                hs = pl.ds(n * HID, HID)
                act_a[yb, kb, :, hs] = v[0:48]
                act_b[yb, kb, :, hs] = v[48:96]
                act_c[kb, yb, :, hs] = v[96:128]
            return carry

        lax.fori_loop(0, 4, body, 0)

    done(g2y[2])
    by_column(col(2), C2)
    finish(y)
    finish(row(1))
    finish(row(3))
    done(g1z[2])
    by_row(row(2), C1)
    done(g3x[2])
    by_row(row(2), QC)
    finish(row(2))
    links.wait(swap_down, DW.at[:, pl.ds(HID, HID)], peer)
    links.drain()


class Reduce:
    def __init__(self, links, part, bufs, nb, i, add, add3):
        self.links, self.part, self.bufs, self.nb, self.i = links, part, bufs, nb, i
        self.add, self.add3 = add, add3
        self.s = [links.slot() for _ in range(6)]

    def t(self, d):
        return (self.i + d + 4) % 4

    def first(self):
        l, p, b, s = self.links, self.part, self.bufs, self.s
        l.start(s[0], p(self.t(2), 0), b(0), self.nb(1))
        l.start(s[1], p(self.t(2), 1), b(1), self.nb(-1))

    def second_right(self):
        self.links.start(self.s[2], self.part(self.t(1), 1), self.bufs(2), self.nb(1))

    def second_left(self):
        self.links.start(self.s[3], self.part(self.t(-1), 0), self.bufs(3), self.nb(-1))

    def third(self):
        l, p, b, s = self.links, self.part, self.bufs, self.s
        l.wait(s[0], b(0), self.nb(-1))
        self.add(p(self.t(1), 0), b(0))
        l.start(s[4], p(self.t(1), 0), b(4), self.nb(1))
        l.wait(s[1], b(1), self.nb(1))
        self.add(p(self.t(-1), 1), b(1))
        l.start(s[5], p(self.t(-1), 1), b(5), self.nb(-1))

    def last(self):
        l, p, b, s = self.links, self.part, self.bufs, self.s
        l.wait(s[3], b(3), self.nb(1))
        l.wait(s[4], b(4), self.nb(-1))
        self.add3(p(self.i, 0), b(3), b(4))
        l.wait(s[2], b(2), self.nb(-1))
        l.wait(s[5], b(5), self.nb(1))
        self.add3(p(self.i, 1), b(2), b(5))


def reduce_phase(me, links, act, DW, S, bufs, F, E, G, out, PA, PB, PC):
    x, y, k = me.x, me.y, me.k
    act_a, act_b, act_c = act
    (A1, A2, A3, A4), (B1, B2, B3, B4), (CC1, CC2, CC3, CC4) = bufs

    def add2d(dst, a):
        dst[...] = (dst[...].astype(F32) + a[...].astype(F32)).astype(BF16)

    def add3_2d(dst, a, b):
        dst[...] = (dst[...].astype(F32) + a[...].astype(F32) + b[...].astype(F32)).astype(BF16)

    def add3d(dst, a):
        lax.fori_loop(0, dst.shape[0], lambda n, t: (add2d(dst.at[n], a.at[n]), t)[1], 0)

    def add3_3d(dst, a, b):
        lax.fori_loop(0, dst.shape[0], lambda n, t: (add3_2d(dst.at[n], a.at[n], b.at[n]), t)[1], 0)

    def add4d(dst, a):
        w = dst.shape[1]
        lax.fori_loop(0, dst.shape[0] * w, lambda n, t: (add2d(dst.at[n // w, n % w], a.at[n // w, n % w]), t)[1], 0)

    def add3_4d(dst, a, b):
        w = dst.shape[1]
        lax.fori_loop(
            0, dst.shape[0] * w,
            lambda n, t: (add3_2d(dst.at[n // w, n % w], a.at[n // w, n % w], b.at[n // w, n % w]), t)[1], 0)

    NS = ((0, 256), (256, 256), (512, 256), (768, 128))

    def shared(xx, off, rows):
        return S[xx, off:off + rows, :].astype(F32)

    def down_a(t):
        def body(m, carry):
            lhs = act_a[pl.ds(2 * m, 2)].reshape(8 * 48, 512)
            for lo, w in NS:
                r = jnp.dot(lhs, DW[t, :, lo:lo + w], preferred_element_type=F32)
                PA[t, pl.ds(2 * m, 2), :, :, lo:lo + w] = r.astype(BF16).reshape(2, 4, 48, w)
            return carry
        lax.fori_loop(0, 2, body, 0)
        PA[t, y, k] = (PA[t, y, k].astype(F32) + shared(t, 0, 48)).astype(BF16)

    def down_b(t):
        def body(xx, carry):
            lhs = act_b[t].reshape(4 * 48, 512)
            for lo, w in NS:
                r = jnp.dot(lhs, DW[xx, :, lo:lo + w], preferred_element_type=F32)
                PB[t, :, xx, :, lo:lo + w] = r.astype(BF16).reshape(4, 48, w)
            return carry
        lax.fori_loop(0, 4, body, 0)

    def down_c(t):
        def body(xx, carry):
            lhs = act_c[t].reshape(4 * 32, 512)
            for lo, w in NS:
                r = jnp.dot(lhs, DW[xx, :, lo:lo + w], preferred_element_type=F32)
                PC[t, xx, :, :, lo:lo + w] = r.astype(BF16).reshape(4, 32, w)
            return carry
        lax.fori_loop(0, 4, body, 0)

    def two(h):
        return pl.ds(2 * h, 2)

    def part_rows(p, h):
        return pl.ds(0, SPLIT[p]) if h == 0 else pl.ds(SPLIT[p], ROWS[p] - SPLIT[p])

    def last_bufs(p, pair):
        return lambda n: pair[0].at[n // 2] if n in (0, 3, 4) else pair[1].at[n // 2]

    ra = Reduce(links, lambda t, h: PA.at[t, two(h)], lambda n: A1.at[n], me.xn, x, add4d, add3_4d)
    rb = Reduce(links, lambda t, h: PB.at[t, two(h)], lambda n: B1.at[n], me.yn, y, add4d, add3_4d)
    rc = Reduce(links, lambda t, h: PC.at[t, two(h)], lambda n: CC1.at[n], me.zn, k, add4d, add3_4d)
    down_b((y + 2) % 4)
    rb.first()
    down_a((x + 2) % 4)
    ra.first()
    down_c((k + 2) % 4)
    rc.first()
    down_b((y + 1) % 4)
    rb.second_right()
    down_b((y + 3) % 4)
    rb.second_left()
    down_a((x + 1) % 4)
    ra.second_right()
    down_a((x + 3) % 4)
    ra.second_left()
    down_c((k + 1) % 4)
    rc.second_right()
    down_c((k + 3) % 4)
    rc.second_left()
    rc.third()
    rb.third()
    ra.third()
    down_a(x)
    down_b(y)
    down_c(k)

    def own_shared(xx, carry):
        PB[y, k, xx] = (PB[y, k, xx].astype(F32) + shared(xx, 48, 48)).astype(BF16)
        PC[k, xx, y] = (PC[k, xx, y].astype(F32) + shared(xx, 96, 32)).astype(BF16)
        return carry

    lax.fori_loop(0, 4, own_shared, 0)

    sa = Reduce(links, lambda t, h: PA.at[x, t, two(h)], lambda n: A2.at[n], me.yn, y, add3d, add3_3d)
    sb = Reduce(links, lambda t, h: PB.at[y, t, two(h)], lambda n: B2.at[n], me.zn, k, add3d, add3_3d)
    sc = Reduce(links, lambda t, h: PC.at[k, t, two(h)], lambda n: CC2.at[n], me.xn, x, add3d, add3_3d)
    ta = Reduce(links, lambda t, h: PA.at[x, y, t, part_rows(0, h)], last_bufs(0, (A3, A4)), me.zn, k, add2d, add3_2d)
    tb = Reduce(links, lambda t, h: PB.at[y, k, t, part_rows(1, h)], last_bufs(1, (B3, B4)), me.xn, x, add2d, add3_2d)
    tc = Reduce(links, lambda t, h: PC.at[k, x, t, part_rows(2, h)], last_bufs(2, (CC3, CC4)), me.yn, y, add2d, add3_2d)

    def enter(before, after):
        before.last()
        after.first()
        after.second_right()
        after.second_left()

    enter(rc, sc)
    enter(ra, sa)
    enter(rb, sb)
    sc.third()
    sa.third()
    sb.third()
    enter(sc, tc)
    enter(sa, ta)
    enter(sb, tb)
    tc.third()
    ta.third()
    tb.third()
    low = me.zh == 0
    far = me.zn(4)

    def exchange(own, p, F):
        rows = pl.ds(OFFS[p], ROWS[p])
        whole = own[...]
        lo = whole[:, 0:448].astype(F32)
        hi = whole[:, 448:896].astype(F32)
        E[rows] = jnp.where(low, hi, lo).astype(BF16)
        F[rows] = jnp.where(low, lo, hi)
        slot = links.slot()
        links.start(slot, E.at[rows], G.at[rows], far)
        return slot

    tc.last()
    slot_c = exchange(PC.at[k, x, y], 2, F)
    ta.last()
    slot_a = exchange(PA.at[x, y, k], 0, F)
    tb.last()
    slot_b = exchange(PB.at[y, k, x], 1, F)
    for p, slot in ((2, slot_c), (0, slot_a), (1, slot_b)):
        rows = pl.ds(OFFS[p], ROWS[p])
        links.wait(slot, G.at[rows], far)
        out[rows] = (F[rows] + G[rows].astype(F32)).astype(BF16)
    links.drain()


def layer_body(tokens, ids, rw, swap, gate, up, down, sgate, sup, sdown, out,
               act_a, act_b, act_c, DW, S, A1, A2, A3, A4, B1, B2, B3, B4, CC1, CC2, CC3, CC4, F, E, G,
               send_sem, recv_sem, local_sem, wt_send, wt_recv):
    me = Place()
    links = Links(send_sem, recv_sem)
    act = (act_a, act_b, act_c)
    vmem = pltpu.VMEM
    pl.run_scoped(
        functools.partial(gather_phase, me, links, tokens, ids, rw, swap, gate, up, down, sgate, sup, sdown, act, DW, S,
                          (local_sem, wt_send, wt_recv)),
        vmem((4, 4, TOK, D), BF16), vmem((4, D, HID), BF16), vmem((D, HID), BF16), vmem((HID, D), BF16),
        vmem((4, 4, 4, TOK, HID), F32), vmem((16, 8, TOK), F32), vmem((16, 8, TOK), F32), vmem((TOK, D), BF16))
    pl.run_scoped(
        functools.partial(reduce_phase, me, links, act, DW, S,
                          ((A1, A2, A3, A4), (B1, B2, B3, B4), (CC1, CC2, CC3, CC4)), F, E, G, out),
        vmem((4, 4, 4, 48, XC), BF16), vmem((4, 4, 4, 48, XC), BF16), vmem((4, 4, 4, 32, XC), BF16))


VM = pl.BlockSpec(memory_space=pltpu.VMEM)
ANY = pl.BlockSpec(memory_space=pl.ANY)


def local(tokens, expert_ids, route_weight, pair_swap, expert_gate, expert_up, expert_down,
          shared_gate, shared_up, shared_down):
    shape = jax.ShapeDtypeStruct
    scratch = pltpu.VMEM
    dma = pltpu.SemaphoreType.DMA
    return pl.pallas_call(
        layer_body,
        name="expert_layer",
        out_shape=shape((TOK, 448), BF16),
        in_specs=[ANY, VM, VM, pl.BlockSpec(memory_space=pltpu.SMEM), ANY, ANY, ANY, ANY, ANY, ANY],
        out_specs=VM,
        scratch_shapes=[
            scratch((4, 4, 48, 512), BF16), scratch((4, 4, 48, 512), BF16), scratch((4, 4, 32, 512), BF16),
            scratch((4, 512, XC), BF16), scratch((4, TOK, XC), BF16),
            scratch((6, 2, 4, 48, XC), BF16), scratch((6, 2, 48, XC), BF16),
            scratch((3, 32, XC), BF16), scratch((3, 16, XC), BF16),
            scratch((6, 2, 4, 48, XC), BF16), scratch((6, 2, 48, XC), BF16),
            scratch((3, 32, XC), BF16), scratch((3, 16, XC), BF16),
            scratch((6, 2, 4, 32, XC), BF16), scratch((6, 2, 32, XC), BF16),
            scratch((3, 16, XC), BF16), scratch((3, 16, XC), BF16),
            scratch((TOK, 448), F32), scratch((TOK, 448), BF16), scratch((TOK, 448), BF16),
            dma((192,)), dma((192,)), dma((8,)), dma((16,)), dma((16,)),
        ],
        compiler_params=pltpu.CompilerParams(collective_id=0, has_side_effects=True, vmem_limit_bytes=63 << 20),
    )(tokens, expert_ids.T, route_weight.T, pair_swap, expert_gate[0], expert_up[0], expert_down[0], shared_gate, shared_up, shared_down)


def solution(mesh):
    in_specs = (
        P("expert", None),
        P("expert", None),
        P("expert", None),
        P(),
        P("expert", None, "dp"),
        P("expert", None, "dp"),
        P("expert", "dp", None),
        P(None, "dp"),
        P(None, "dp"),
        P("dp", None),
    )
    return jax.shard_map(local, mesh=mesh, in_specs=in_specs, out_specs=P("expert", "dp"), check_vma=False)
```

```python
import functools

import jax
import jax.numpy as jnp
from jax import lax
from jax.experimental import pallas as pl
from jax.experimental.pallas import tpu as pltpu
from jax.sharding import PartitionSpec as P

MESH = pl.DeviceIdType.MESH
F32 = jnp.float32
BF16 = jnp.bfloat16
routed_scale = 2.5
D = 3584
TOK = 128
HID = 256
C2 = (0, 1152)
C1 = (1152, 896)
QBASE, QW = 2048, 384
ROWS = (48, 48, 32)
OFFS = (0, 48, 96)
XC = 896
SPLIT = (32, 32, 16)


class Place:
    def __init__(self):
        self.dp = lax.axis_index("dp")
        self.ex = lax.axis_index("expert")
        self.x = self.dp % 4
        self.zh = self.dp // 4
        self.y = self.ex // 8
        self.k = (self.ex // 2) % 4
        self.c = self.ex % 2
        self.z = self.zh * 4 + self.k

    def xn(self, d):
        return (self.zh * 4 + (self.x + d + 4) % 4, self.ex)

    def yn(self, d):
        return (self.dp, ((self.y + d + 4) % 4) * 8 + self.k * 2 + self.c)

    def zn(self, d):
        z = (self.z + d + 8) % 8
        return ((z // 4) * 4 + self.x, self.y * 8 + (z % 4) * 2 + self.c)

    def peer(self):
        return (self.dp, self.ex + 1 - 2 * self.c)

    def plane(self, q):
        return (self.dp, q * 2 + self.c)


class Links:
    def __init__(self, send_sem, recv_sem):
        self.send_sem, self.recv_sem, self.count = send_sem, recv_sem, 0
        self.sent = []

    def slot(self):
        self.count += 1
        return self.count - 1

    def start(self, slot, src, dst, dev):
        copy = pltpu.make_async_remote_copy(
            src_ref=src, dst_ref=dst, send_sem=self.send_sem.at[slot], recv_sem=self.recv_sem.at[slot],
            device_id=dev, device_id_type=MESH)
        copy.start()
        self.sent.append(copy)

    def wait(self, slot, dst, dev):
        pltpu.make_async_remote_copy(
            src_ref=dst, dst_ref=dst, send_sem=self.send_sem.at[slot], recv_sem=self.recv_sem.at[slot],
            device_id=dev, device_id_type=MESH).wait_recv()

    def drain(self):
        for copy in self.sent:
            copy.wait_send()
        self.sent = []


class Gather:
    def __init__(self, links, unit, nb, i, own=None):
        self.links, self.unit, self.nb, self.i = links, unit, nb, i
        self.own = own or (lambda h: unit(i, h))
        self.s = [links.slot() for _ in range(6)]

    def send(self):
        l, u, i, s, nb = self.links, self.unit, self.i, self.s, self.nb
        l.start(s[0], self.own(0), u(i, 0), nb(1))
        l.start(s[1], self.own(1), u(i, 1), nb(-1))
        l.start(s[2], self.own(1), u(i, 1), nb(1))
        l.start(s[3], self.own(0), u(i, 0), nb(-1))

    def forward(self):
        l, u, s, nb = self.links, self.unit, self.s, self.nb
        left, right = (self.i + 3) % 4, (self.i + 1) % 4
        l.wait(s[0], u(left, 0), nb(-1))
        l.start(s[4], u(left, 0), u(left, 0), nb(1))
        l.wait(s[1], u(right, 1), nb(1))
        l.start(s[5], u(right, 1), u(right, 1), nb(-1))

    def near(self):
        l, u, s, nb = self.links, self.unit, self.s, self.nb
        left, right = (self.i + 3) % 4, (self.i + 1) % 4
        l.wait(s[2], u(left, 1), nb(-1))
        l.wait(s[3], u(right, 0), nb(1))

    def far(self):
        l, u, s, nb = self.links, self.unit, self.s, self.nb
        opp = (self.i + 2) % 4
        l.wait(s[4], u(opp, 0), nb(-1))
        l.wait(s[5], u(opp, 1), nb(1))


def greet(devices):
    barrier = pltpu.get_barrier_semaphore()
    for dev in devices:
        pl.semaphore_signal(barrier, inc=1, device_id=dev, device_id_type=MESH)
    pl.semaphore_wait(barrier, len(devices))


def gather_phase(me, links, tokens, ids, rw, swap, gate, up, down, sgate, sup, sdown, act, DW, S, sem,
                 X, W, SW, RAW, acc, WT, wt):
    x, y, k = me.x, me.y, me.k
    q_me = y * 4 + k
    c1 = pl.ds(C1[0], C1[1])
    c2 = pl.ds(C2[0], C2[1])
    act_a, act_b, act_c = act
    local_sem, wt_send, wt_recv = sem

    def qcol(u):
        return pl.ds(pl.multiple_of(QBASE + QW * u, 128), QW)

    qx = qcol(x)

    def load(src, dst, n):
        copy = pltpu.make_async_copy(src, dst, local_sem.at[n])
        copy.start()
        return copy

    own = load(tokens, X.at[y, k], 0)
    w_gate = load(gate, W.at[0], 2)
    w_up = load(up, W.at[2], 3)
    w_down = load(down, RAW, 4)
    w_sg = load(sgate, SW, 5)

    hops = [me.plane((q_me + d) % 16) for d in range(1, 16)]
    greet(hops + [me.xn(1), me.xn(-1), me.yn(1), me.yn(-1), me.zn(1), me.zn(-1), me.zn(4), me.peer()])

    def rows(h):
        return pl.ds(64 * h, 64)

    def two(h):
        return pl.ds(2 * h, 2)

    def row(d):
        return (y + d) % 4

    def col(d):
        return (k + d) % 4

    part = functools.partial
    g3y = Gather(links, lambda u, h: X.at[u, k, rows(h), qx], me.yn, y, lambda h: tokens.at[rows(h), qx])
    g1y = Gather(links, lambda u, h: X.at[u, k, rows(h), c1], me.yn, y, lambda h: tokens.at[rows(h), c1])
    g2z = Gather(links, lambda u, h: X.at[y, u, rows(h), c2], me.zn, k, lambda h: tokens.at[rows(h), c2])
    g3z = [Gather(links, part(lambda s, u, h: X.at[s, u, rows(h), qx], row(d)), me.zn, k,
                  (lambda h: tokens.at[rows(h), qx]) if d == 0 else None) for d in range(4)]
    g1z = [Gather(links, part(lambda s, u, h: X.at[s, u, rows(h), c1], row(d)), me.zn, k,
                  (lambda h: tokens.at[rows(h), c1]) if d == 0 else None) for d in range(4)]
    g2y = [Gather(links, part(lambda s, u, h: X.at[u, s, rows(h), c2], col(d)), me.yn, y,
                  (lambda h: tokens.at[rows(h), c2]) if d == 0 else None) for d in range(4)]
    g3x0 = {d: Gather(links, part(lambda s, u, h: X.at[y, s, rows(h), qcol(u)], col(d)), me.xn, x) for d in (1, 3, 2)}
    g3x = {d: Gather(links, part(lambda s, u, h: X.at[s, two(h), :, qcol(u)], row(d)), me.xn, x) for d in (1, 3, 2)}

    def done(g):
        g.near()
        g.far()

    def dots(read, write, cols):
        lo, width = cols

        def step(n, carry):
            write(n, jnp.dot(read(lo, width), W[n, lo:lo + width, :], preferred_element_type=F32))
            return carry

        lax.fori_loop(0, 4, step, 0)

    def by_column(s, cols):
        def write(n, res):
            acc[n, :, s] += res.reshape(4, TOK, HID)

        dots(lambda lo, width: X[:, s, :, lo:lo + width].reshape(4 * TOK, width), write, cols)

    def by_row(u, cols):
        def write(n, res):
            acc[n, u] += res.reshape(4, TOK, HID)

        dots(lambda lo, width: X[u, :, :, lo:lo + width].reshape(4 * TOK, width), write, cols)

    QC = (QBASE, D - QBASE)
    RC = (C1[0], D - C1[0])

    g3z[0].send()
    g3y.send()
    peer = me.peer()
    swap_gate, swap_up, swap_down = links.slot(), links.slot(), links.slot()
    links.start(swap_gate, gate, W.at[1], peer)
    links.start(swap_up, up, W.at[3], peer)
    weight = rw[...]
    mix = routed_scale * (weight / jnp.sum(weight, axis=0, keepdims=True))
    chosen = ids[...]
    lane_row = lax.broadcasted_iota(jnp.int32, (8, TOK), 0)
    for q in range(16):
        tile = jnp.zeros((8, TOK), F32)
        for r, column in enumerate((2 * q + me.c, 2 * q + 1 - me.c)):
            stored = (column + 16 * swap[column % 16]) % 32
            picked = jnp.sum(jnp.where(chosen == stored, mix, 0.0), axis=0, keepdims=True)
            tile = jnp.where(lane_row == r, picked, tile)
        wt[q] = tile
    own.wait()
    g3z[0].forward()
    g3y.forward()
    g3z[0].near()
    g3x0[1].send()
    g3x0[3].send()
    g1y.send()
    g3y.near()
    g3z[1].send()
    g3z[3].send()
    g3z[0].far()
    g3x0[2].send()
    g3y.far()
    g3z[2].send()
    g2y[0].send()
    for d in range(1, 16):
        q = (q_me + d) % 16
        pltpu.make_async_remote_copy(
            src_ref=wt.at[q], dst_ref=WT.at[q_me], send_sem=wt_send.at[d], recv_sem=wt_recv.at[d],
            device_id=me.plane(q), device_id_type=MESH).start()
    WT[q_me] = wt[q_me]
    g3z[1].forward()
    g3z[3].forward()
    g2z.send()
    g3z[2].forward()
    g1z[0].send()
    w_sg.wait()
    sg = jnp.dot(X[y, k], SW[...], preferred_element_type=F32)
    w_su = load(sup, SW, 5)
    silu = sg / (1.0 + jnp.exp(-sg))
    for d in (1, 3, 2):
        g3x0[d].forward()
    g1y.forward()
    done(g3z[1])
    g3x[1].send()
    g2z.forward()
    g1y.near()
    g1z[1].send()
    g1y.far()
    w_down.wait()
    for xx in range(4):
        DW[xx, 0:HID] = jnp.concatenate(
            [RAW[:, 448 * xx:448 * xx + 448], RAW[:, 1792 + 448 * xx:1792 + 448 * xx + 448]], axis=1)
    links.start(swap_down, DW.at[:, pl.ds(0, HID)], DW.at[:, pl.ds(HID, HID)], peer)
    w_sdown = load(sdown, RAW, 4)
    done(g3z[3])
    done(g3z[2])
    g2z.near()
    g2y[1].send()
    g2y[0].forward()
    g3x[1].forward()
    g3x[3].send()
    w_su.wait()
    sact = (silu * jnp.dot(X[y, k], SW[...], preferred_element_type=F32)).astype(BF16)
    g2z.far()
    g1z[0].forward()
    g1z[3].send()
    acc[...] = jnp.zeros_like(acc)
    w_gate.wait()
    w_up.wait()
    links.wait(swap_gate, W.at[1], peer)
    links.wait(swap_up, W.at[3], peer)
    done(g2y[0])
    by_column(k, C2)
    g2y[1].forward()
    g2y[3].send()
    g3x[3].forward()
    g3x[2].send()
    for d in (1, 3, 2):
        done(g3x0[d])
    done(g1z[0])
    by_row(y, RC)
    g1z[1].forward()
    g1z[2].send()
    done(g2y[1])
    by_column(col(1), C2)
    g2y[3].forward()
    g2y[2].send()
    w_sdown.wait()
    for xx in range(4):
        S[xx] = jnp.concatenate(
            [jnp.dot(sact, RAW[:, base + 448 * xx:base + 448 * xx + 448], preferred_element_type=F32)
             for base in (0, 1792)], axis=1).astype(BF16)
    g1z[3].forward()
    done(g3x[1])
    done(g1z[1])
    by_row(row(1), RC)
    g2y[2].forward()
    g3x[2].forward()
    done(g2y[3])
    by_column(col(3), C2)
    g1z[2].forward()
    done(g3x[3])
    done(g1z[3])
    by_row(row(3), RC)
    for d in range(1, 16):
        q = (q_me + 16 - d) % 16
        pltpu.make_async_remote_copy(
            src_ref=wt.at[q], dst_ref=WT.at[q], send_sem=wt_send.at[d], recv_sem=wt_recv.at[d],
            device_id=me.plane(q), device_id_type=MESH).wait()

    def finish(yb):
        def body(kb, carry):
            w = jnp.transpose(WT[yb * 4 + kb])
            for n in range(2):
                g = acc[n, yb, kb]
                u = acc[2 + n, yb, kb]
                v = (g / (1.0 + jnp.exp(-g)) * u * w[:, n:n + 1]).astype(BF16)
                hs = pl.ds(n * HID, HID)
                act_a[yb, kb, :, hs] = v[0:48]
                act_b[yb, kb, :, hs] = v[48:96]
                act_c[kb, yb, :, hs] = v[96:128]
            return carry

        lax.fori_loop(0, 4, body, 0)

    done(g2y[2])
    by_column(col(2), C2)
    finish(y)
    finish(row(1))
    finish(row(3))
    done(g1z[2])
    by_row(row(2), C1)
    done(g3x[2])
    by_row(row(2), QC)
    finish(row(2))
    links.wait(swap_down, DW.at[:, pl.ds(HID, HID)], peer)
    links.drain()


class Reduce:
    def __init__(self, links, part, bufs, nb, i, add, add3):
        self.links, self.part, self.bufs, self.nb, self.i = links, part, bufs, nb, i
        self.add, self.add3 = add, add3
        self.s = [links.slot() for _ in range(6)]

    def t(self, d):
        return (self.i + d + 4) % 4

    def first(self):
        l, p, b, s = self.links, self.part, self.bufs, self.s
        l.start(s[0], p(self.t(2), 0), b(0), self.nb(1))
        l.start(s[1], p(self.t(2), 1), b(1), self.nb(-1))

    def second_right(self):
        self.links.start(self.s[2], self.part(self.t(1), 1), self.bufs(2), self.nb(1))

    def second_left(self):
        self.links.start(self.s[3], self.part(self.t(-1), 0), self.bufs(3), self.nb(-1))

    def third(self):
        l, p, b, s = self.links, self.part, self.bufs, self.s
        l.wait(s[0], b(0), self.nb(-1))
        self.add(p(self.t(1), 0), b(0))
        l.start(s[4], p(self.t(1), 0), b(4), self.nb(1))
        l.wait(s[1], b(1), self.nb(1))
        self.add(p(self.t(-1), 1), b(1))
        l.start(s[5], p(self.t(-1), 1), b(5), self.nb(-1))

    def last(self):
        l, p, b, s = self.links, self.part, self.bufs, self.s
        l.wait(s[3], b(3), self.nb(1))
        l.wait(s[4], b(4), self.nb(-1))
        self.add3(p(self.i, 0), b(3), b(4))
        l.wait(s[2], b(2), self.nb(-1))
        l.wait(s[5], b(5), self.nb(1))
        self.add3(p(self.i, 1), b(2), b(5))


def reduce_phase(me, links, act, DW, S, bufs, F, E, G, out, PA, PB, PC):
    x, y, k = me.x, me.y, me.k
    act_a, act_b, act_c = act
    (A1, A2, A3, A4), (B1, B2, B3, B4), (CC1, CC2, CC3, CC4) = bufs

    def add2d(dst, a):
        dst[...] = (dst[...].astype(F32) + a[...].astype(F32)).astype(BF16)

    def add3_2d(dst, a, b):
        dst[...] = (dst[...].astype(F32) + a[...].astype(F32) + b[...].astype(F32)).astype(BF16)

    def add3d(dst, a):
        lax.fori_loop(0, dst.shape[0], lambda n, t: (add2d(dst.at[n], a.at[n]), t)[1], 0)

    def add3_3d(dst, a, b):
        lax.fori_loop(0, dst.shape[0], lambda n, t: (add3_2d(dst.at[n], a.at[n], b.at[n]), t)[1], 0)

    def add4d(dst, a):
        w = dst.shape[1]
        lax.fori_loop(0, dst.shape[0] * w, lambda n, t: (add2d(dst.at[n // w, n % w], a.at[n // w, n % w]), t)[1], 0)

    def add3_4d(dst, a, b):
        w = dst.shape[1]
        lax.fori_loop(
            0, dst.shape[0] * w,
            lambda n, t: (add3_2d(dst.at[n // w, n % w], a.at[n // w, n % w], b.at[n // w, n % w]), t)[1], 0)

    NS = ((0, 256), (256, 256), (512, 256), (768, 128))

    def shared(xx, off, rows):
        return S[xx, off:off + rows, :].astype(F32)

    def down_a(t):
        def body(m, carry):
            lhs = act_a[pl.ds(2 * m, 2)].reshape(8 * 48, 512)
            for lo, w in NS:
                r = jnp.dot(lhs, DW[t, :, lo:lo + w], preferred_element_type=F32)
                PA[t, pl.ds(2 * m, 2), :, :, lo:lo + w] = r.astype(BF16).reshape(2, 4, 48, w)
            return carry
        lax.fori_loop(0, 2, body, 0)
        PA[t, y, k] = (PA[t, y, k].astype(F32) + shared(t, 0, 48)).astype(BF16)

    def down_b(t):
        def body(xx, carry):
            lhs = act_b[t].reshape(4 * 48, 512)
            for lo, w in NS:
                r = jnp.dot(lhs, DW[xx, :, lo:lo + w], preferred_element_type=F32)
                PB[t, :, xx, :, lo:lo + w] = r.astype(BF16).reshape(4, 48, w)
            return carry
        lax.fori_loop(0, 4, body, 0)

    def down_c(t):
        def body(xx, carry):
            lhs = act_c[t].reshape(4 * 32, 512)
            for lo, w in NS:
                r = jnp.dot(lhs, DW[xx, :, lo:lo + w], preferred_element_type=F32)
                PC[t, xx, :, :, lo:lo + w] = r.astype(BF16).reshape(4, 32, w)
            return carry
        lax.fori_loop(0, 4, body, 0)

    def two(h):
        return pl.ds(2 * h, 2)

    def part_rows(p, h):
        return pl.ds(0, SPLIT[p]) if h == 0 else pl.ds(SPLIT[p], ROWS[p] - SPLIT[p])

    def last_bufs(p, pair):
        return lambda n: pair[0].at[n // 2] if n in (0, 3, 4) else pair[1].at[n // 2]

    ra = Reduce(links, lambda t, h: PA.at[t, two(h)], lambda n: A1.at[n], me.xn, x, add4d, add3_4d)
    rb = Reduce(links, lambda t, h: PB.at[t, two(h)], lambda n: B1.at[n], me.yn, y, add4d, add3_4d)
    rc = Reduce(links, lambda t, h: PC.at[t, two(h)], lambda n: CC1.at[n], me.zn, k, add4d, add3_4d)
    down_b((y + 2) % 4)
    rb.first()
    down_a((x + 2) % 4)
    ra.first()
    down_c((k + 2) % 4)
    rc.first()
    down_b((y + 1) % 4)
    rb.second_right()
    down_b((y + 3) % 4)
    rb.second_left()
    down_a((x + 1) % 4)
    ra.second_right()
    down_a((x + 3) % 4)
    ra.second_left()
    down_c((k + 1) % 4)
    rc.second_right()
    down_c((k + 3) % 4)
    rc.second_left()
    rc.third()
    rb.third()
    ra.third()
    down_a(x)
    down_b(y)
    down_c(k)

    def own_shared(xx, carry):
        PB[y, k, xx] = (PB[y, k, xx].astype(F32) + shared(xx, 48, 48)).astype(BF16)
        PC[k, xx, y] = (PC[k, xx, y].astype(F32) + shared(xx, 96, 32)).astype(BF16)
        return carry

    lax.fori_loop(0, 4, own_shared, 0)

    sa = Reduce(links, lambda t, h: PA.at[x, t, two(h)], lambda n: A2.at[n], me.yn, y, add3d, add3_3d)
    sb = Reduce(links, lambda t, h: PB.at[y, t, two(h)], lambda n: B2.at[n], me.zn, k, add3d, add3_3d)
    sc = Reduce(links, lambda t, h: PC.at[k, t, two(h)], lambda n: CC2.at[n], me.xn, x, add3d, add3_3d)
    ta = Reduce(links, lambda t, h: PA.at[x, y, t, part_rows(0, h)], last_bufs(0, (A3, A4)), me.zn, k, add2d, add3_2d)
    tb = Reduce(links, lambda t, h: PB.at[y, k, t, part_rows(1, h)], last_bufs(1, (B3, B4)), me.xn, x, add2d, add3_2d)
    tc = Reduce(links, lambda t, h: PC.at[k, x, t, part_rows(2, h)], last_bufs(2, (CC3, CC4)), me.yn, y, add2d, add3_2d)

    def enter(before, after):
        before.last()
        after.first()
        after.second_right()
        after.second_left()

    enter(rc, sc)
    enter(ra, sa)
    enter(rb, sb)
    sc.third()
    sa.third()
    sb.third()
    enter(sc, tc)
    enter(sa, ta)
    enter(sb, tb)
    tc.third()
    ta.third()
    tb.third()
    low = me.zh == 0
    far = me.zn(4)

    def exchange(own, p, F):
        rows = pl.ds(OFFS[p], ROWS[p])
        whole = own[...]
        lo = whole[:, 0:448].astype(F32)
        hi = whole[:, 448:896].astype(F32)
        E[rows] = jnp.where(low, hi, lo).astype(BF16)
        F[rows] = jnp.where(low, lo, hi)
        slot = links.slot()
        links.start(slot, E.at[rows], G.at[rows], far)
        return slot

    tc.last()
    slot_c = exchange(PC.at[k, x, y], 2, F)
    ta.last()
    slot_a = exchange(PA.at[x, y, k], 0, F)
    tb.last()
    slot_b = exchange(PB.at[y, k, x], 1, F)
    for p, slot in ((2, slot_c), (0, slot_a), (1, slot_b)):
        rows = pl.ds(OFFS[p], ROWS[p])
        links.wait(slot, G.at[rows], far)
        out[rows] = (F[rows] + G[rows].astype(F32)).astype(BF16)
    links.drain()


def layer_body(tokens, ids, rw, swap, gate, up, down, sgate, sup, sdown, out,
               act_a, act_b, act_c, DW, S, A1, A2, A3, A4, B1, B2, B3, B4, CC1, CC2, CC3, CC4, F, E, G,
               send_sem, recv_sem, local_sem, wt_send, wt_recv):
    me = Place()
    links = Links(send_sem, recv_sem)
    act = (act_a, act_b, act_c)
    vmem = pltpu.VMEM
    pl.run_scoped(
        functools.partial(gather_phase, me, links, tokens, ids, rw, swap, gate, up, down, sgate, sup, sdown, act, DW, S,
                          (local_sem, wt_send, wt_recv)),
        vmem((4, 4, TOK, D), BF16), vmem((4, D, HID), BF16), vmem((D, HID), BF16), vmem((HID, D), BF16),
        vmem((4, 4, 4, TOK, HID), F32), vmem((16, 8, TOK), F32), vmem((16, 8, TOK), F32))
    pl.run_scoped(
        functools.partial(reduce_phase, me, links, act, DW, S,
                          ((A1, A2, A3, A4), (B1, B2, B3, B4), (CC1, CC2, CC3, CC4)), F, E, G, out),
        vmem((4, 4, 4, 48, XC), BF16), vmem((4, 4, 4, 48, XC), BF16), vmem((4, 4, 4, 32, XC), BF16))


VM = pl.BlockSpec(memory_space=pltpu.VMEM)
ANY = pl.BlockSpec(memory_space=pl.ANY)


def local(tokens, expert_ids, route_weight, pair_swap, expert_gate, expert_up, expert_down,
          shared_gate, shared_up, shared_down):
    shape = jax.ShapeDtypeStruct
    scratch = pltpu.VMEM
    dma = pltpu.SemaphoreType.DMA
    return pl.pallas_call(
        layer_body,
        name="expert_layer",
        out_shape=shape((TOK, 448), BF16),
        in_specs=[ANY, VM, VM, pl.BlockSpec(memory_space=pltpu.SMEM), ANY, ANY, ANY, ANY, ANY, ANY],
        out_specs=VM,
        scratch_shapes=[
            scratch((4, 4, 48, 512), BF16), scratch((4, 4, 48, 512), BF16), scratch((4, 4, 32, 512), BF16),
            scratch((4, 512, XC), BF16), scratch((4, TOK, XC), BF16),
            scratch((6, 2, 4, 48, XC), BF16), scratch((6, 2, 48, XC), BF16),
            scratch((3, 32, XC), BF16), scratch((3, 16, XC), BF16),
            scratch((6, 2, 4, 48, XC), BF16), scratch((6, 2, 48, XC), BF16),
            scratch((3, 32, XC), BF16), scratch((3, 16, XC), BF16),
            scratch((6, 2, 4, 32, XC), BF16), scratch((6, 2, 32, XC), BF16),
            scratch((3, 16, XC), BF16), scratch((3, 16, XC), BF16),
            scratch((TOK, 448), F32), scratch((TOK, 448), BF16), scratch((TOK, 448), BF16),
            dma((192,)), dma((192,)), dma((8,)), dma((16,)), dma((16,)),
        ],
        compiler_params=pltpu.CompilerParams(collective_id=0, has_side_effects=True, vmem_limit_bytes=63 << 20),
    )(tokens, expert_ids.T, route_weight.T, pair_swap, expert_gate[0], expert_up[0], expert_down[0], shared_gate, shared_up, shared_down)


def solution(mesh):
    in_specs = (
        P("expert", None),
        P("expert", None),
        P("expert", None),
        P(),
        P("expert", None, "dp"),
        P("expert", None, "dp"),
        P("expert", "dp", None),
        P(None, "dp"),
        P(None, "dp"),
        P("dp", None),
    )
    return jax.shard_map(local, mesh=mesh, in_specs=in_specs, out_specs=P("expert", "dp"), check_vma=False)
```

```python
import functools

import jax
import jax.numpy as jnp
from jax import lax
from jax.experimental import pallas as pl
from jax.experimental.pallas import tpu as pltpu
from jax.sharding import PartitionSpec as P

MESH = pl.DeviceIdType.MESH
F32 = jnp.float32
BF16 = jnp.bfloat16
routed_scale = 2.5
D = 3584
TOK = 128
HID = 256
C2 = (0, 1152)
C1 = (1152, 896)
QBASE, QW = 2048, 384
ROWS = (48, 48, 32)
OFFS = (0, 48, 96)
XC = 896
SPLIT = (32, 32, 16)


class Place:
    def __init__(self):
        self.dp = lax.axis_index("dp")
        self.ex = lax.axis_index("expert")
        self.x = self.dp % 4
        self.zh = self.dp // 4
        self.y = self.ex // 8
        self.k = (self.ex // 2) % 4
        self.c = self.ex % 2
        self.z = self.zh * 4 + self.k

    def xn(self, d):
        return (self.zh * 4 + (self.x + d + 4) % 4, self.ex)

    def yn(self, d):
        return (self.dp, ((self.y + d + 4) % 4) * 8 + self.k * 2 + self.c)

    def zn(self, d):
        z = (self.z + d + 8) % 8
        return ((z // 4) * 4 + self.x, self.y * 8 + (z % 4) * 2 + self.c)

    def peer(self):
        return (self.dp, self.ex + 1 - 2 * self.c)

    def plane(self, q):
        return (self.dp, q * 2 + self.c)


class Links:
    def __init__(self, send_sem, recv_sem):
        self.send_sem, self.recv_sem, self.count = send_sem, recv_sem, 0
        self.sent = []

    def slot(self):
        self.count += 1
        return self.count - 1

    def start(self, slot, src, dst, dev):
        copy = pltpu.make_async_remote_copy(
            src_ref=src, dst_ref=dst, send_sem=self.send_sem.at[slot], recv_sem=self.recv_sem.at[slot],
            device_id=dev, device_id_type=MESH)
        copy.start()
        self.sent.append(copy)

    def wait(self, slot, dst, dev):
        pltpu.make_async_remote_copy(
            src_ref=dst, dst_ref=dst, send_sem=self.send_sem.at[slot], recv_sem=self.recv_sem.at[slot],
            device_id=dev, device_id_type=MESH).wait_recv()

    def drain(self):
        for copy in self.sent:
            copy.wait_send()
        self.sent = []


class Gather:
    def __init__(self, links, unit, nb, i, own=None):
        self.links, self.unit, self.nb, self.i = links, unit, nb, i
        self.own = own or (lambda h: unit(i, h))
        self.s = [links.slot() for _ in range(6)]

    def send(self):
        l, u, i, s, nb = self.links, self.unit, self.i, self.s, self.nb
        l.start(s[0], self.own(0), u(i, 0), nb(1))
        l.start(s[1], self.own(1), u(i, 1), nb(-1))
        l.start(s[2], self.own(1), u(i, 1), nb(1))
        l.start(s[3], self.own(0), u(i, 0), nb(-1))

    def forward(self):
        l, u, s, nb = self.links, self.unit, self.s, self.nb
        left, right = (self.i + 3) % 4, (self.i + 1) % 4
        l.wait(s[0], u(left, 0), nb(-1))
        l.start(s[4], u(left, 0), u(left, 0), nb(1))
        l.wait(s[1], u(right, 1), nb(1))
        l.start(s[5], u(right, 1), u(right, 1), nb(-1))

    def near(self):
        l, u, s, nb = self.links, self.unit, self.s, self.nb
        left, right = (self.i + 3) % 4, (self.i + 1) % 4
        l.wait(s[2], u(left, 1), nb(-1))
        l.wait(s[3], u(right, 0), nb(1))

    def far(self):
        l, u, s, nb = self.links, self.unit, self.s, self.nb
        opp = (self.i + 2) % 4
        l.wait(s[4], u(opp, 0), nb(-1))
        l.wait(s[5], u(opp, 1), nb(1))


def greet(devices):
    barrier = pltpu.get_barrier_semaphore()
    for dev in devices:
        pl.semaphore_signal(barrier, inc=1, device_id=dev, device_id_type=MESH)
    pl.semaphore_wait(barrier, len(devices))


def gather_phase(me, links, tokens, ids, rw, swap, gate, up, down, sgate, sup, sdown, act, DW, S, sem,
                 X, W, SW, RAW, acc, WT, wt):
    x, y, k = me.x, me.y, me.k
    q_me = y * 4 + k
    c1 = pl.ds(C1[0], C1[1])
    c2 = pl.ds(C2[0], C2[1])
    act_a, act_b, act_c = act
    local_sem, wt_send, wt_recv = sem

    def qcol(u):
        return pl.ds(pl.multiple_of(QBASE + QW * u, 128), QW)

    qx = qcol(x)

    def load(src, dst, n):
        copy = pltpu.make_async_copy(src, dst, local_sem.at[n])
        copy.start()
        return copy

    own = load(tokens, X.at[y, k], 0)
    w_gate = load(gate, W.at[0], 2)
    w_up = load(up, W.at[2], 3)
    w_down = load(down, RAW, 4)
    w_sg = load(sgate, SW, 5)

    hops = [me.plane((q_me + d) % 16) for d in range(1, 16)]
    greet(hops + [me.xn(1), me.xn(-1), me.yn(1), me.yn(-1), me.zn(1), me.zn(-1), me.zn(4), me.peer()])

    def rows(h):
        return pl.ds(64 * h, 64)

    def two(h):
        return pl.ds(2 * h, 2)

    def row(d):
        return (y + d) % 4

    def col(d):
        return (k + d) % 4

    part = functools.partial
    g3y = Gather(links, lambda u, h: X.at[u, k, rows(h), qx], me.yn, y, lambda h: tokens.at[rows(h), qx])
    g1y = Gather(links, lambda u, h: X.at[u, k, rows(h), c1], me.yn, y, lambda h: tokens.at[rows(h), c1])
    g2z = Gather(links, lambda u, h: X.at[y, u, rows(h), c2], me.zn, k, lambda h: tokens.at[rows(h), c2])
    g3z = [Gather(links, part(lambda s, u, h: X.at[s, u, rows(h), qx], row(d)), me.zn, k,
                  (lambda h: tokens.at[rows(h), qx]) if d == 0 else None) for d in range(4)]
    g1z = [Gather(links, part(lambda s, u, h: X.at[s, u, rows(h), c1], row(d)), me.zn, k,
                  (lambda h: tokens.at[rows(h), c1]) if d == 0 else None) for d in range(4)]
    g2y = [Gather(links, part(lambda s, u, h: X.at[u, s, rows(h), c2], col(d)), me.yn, y,
                  (lambda h: tokens.at[rows(h), c2]) if d == 0 else None) for d in range(4)]
    g3x0 = {d: Gather(links, part(lambda s, u, h: X.at[y, s, rows(h), qcol(u)], col(d)), me.xn, x) for d in (1, 3, 2)}
    g3x = {d: Gather(links, part(lambda s, u, h: X.at[s, two(h), :, qcol(u)], row(d)), me.xn, x) for d in (1, 3, 2)}

    def done(g):
        g.near()
        g.far()

    def dots(read, write, cols):
        lo, width = cols

        def step(n, carry):
            write(n, jnp.dot(read(lo, width), W[n, lo:lo + width, :], preferred_element_type=F32))
            return carry

        lax.fori_loop(0, 4, step, 0)

    def by_column(s, cols):
        def write(n, res):
            acc[n, :, s] += res.reshape(4, TOK, HID)

        dots(lambda lo, width: X[:, s, :, lo:lo + width].reshape(4 * TOK, width), write, cols)

    def by_row(u, cols):
        def write(n, res):
            acc[n, u] += res.reshape(4, TOK, HID)

        dots(lambda lo, width: X[u, :, :, lo:lo + width].reshape(4 * TOK, width), write, cols)

    QC = (QBASE, D - QBASE)
    RC = (C1[0], D - C1[0])

    g3z[0].send()
    g3y.send()
    peer = me.peer()
    swap_gate, swap_up, swap_down = links.slot(), links.slot(), links.slot()
    links.start(swap_gate, gate, W.at[1], peer)
    links.start(swap_up, up, W.at[3], peer)
    weight = rw[...]
    mix = routed_scale * (weight / jnp.sum(weight, axis=0, keepdims=True))
    chosen = ids[...]
    lane_row = lax.broadcasted_iota(jnp.int32, (8, TOK), 0)
    for q in range(16):
        tile = jnp.zeros((8, TOK), F32)
        for r, column in enumerate((2 * q + me.c, 2 * q + 1 - me.c)):
            stored = (column + 16 * swap[column % 16]) % 32
            picked = jnp.sum(jnp.where(chosen == stored, mix, 0.0), axis=0, keepdims=True)
            tile = jnp.where(lane_row == r, picked, tile)
        wt[q] = tile
    own.wait()
    g3z[0].forward()
    g3y.forward()
    g3z[0].near()
    g3x0[1].send()
    g3x0[3].send()
    g1y.send()
    g3y.near()
    g3z[1].send()
    g3z[3].send()
    g3z[0].far()
    g3x0[2].send()
    g3y.far()
    g3z[2].send()
    g2y[0].send()
    for d in range(1, 16):
        q = (q_me + d) % 16
        pltpu.make_async_remote_copy(
            src_ref=wt.at[q], dst_ref=WT.at[q_me], send_sem=wt_send.at[d], recv_sem=wt_recv.at[d],
            device_id=me.plane(q), device_id_type=MESH).start()
    WT[q_me] = wt[q_me]
    g3z[1].forward()
    g3z[3].forward()
    g2z.send()
    g3z[2].forward()
    g1z[0].send()
    w_sg.wait()
    sg = jnp.dot(X[y, k], SW[...], preferred_element_type=F32)
    w_su = load(sup, SW, 5)
    silu = sg / (1.0 + jnp.exp(-sg))
    for d in (1, 3, 2):
        g3x0[d].forward()
    g1y.forward()
    done(g3z[1])
    g3x[1].send()
    g2z.forward()
    g1y.near()
    g1z[1].send()
    g1y.far()
    w_down.wait()
    for xx in range(4):
        DW[xx, 0:HID] = jnp.concatenate(
            [RAW[:, 448 * xx:448 * xx + 448], RAW[:, 1792 + 448 * xx:1792 + 448 * xx + 448]], axis=1)
    links.start(swap_down, DW.at[:, pl.ds(0, HID)], DW.at[:, pl.ds(HID, HID)], peer)
    w_sdown = load(sdown, RAW, 4)
    done(g3z[3])
    done(g3z[2])
    g2z.near()
    g2y[1].send()
    g2y[0].forward()
    g3x[1].forward()
    g3x[3].send()
    w_su.wait()
    sact = (silu * jnp.dot(X[y, k], SW[...], preferred_element_type=F32)).astype(BF16)
    g2z.far()
    g1z[0].forward()
    g1z[3].send()
    acc[...] = jnp.zeros_like(acc)
    w_gate.wait()
    w_up.wait()
    links.wait(swap_gate, W.at[1], peer)
    links.wait(swap_up, W.at[3], peer)
    done(g2y[0])
    by_column(k, C2)
    g2y[1].forward()
    g2y[3].send()
    g3x[3].forward()
    g3x[2].send()
    for d in (1, 3, 2):
        done(g3x0[d])
    done(g1z[0])
    by_row(y, RC)
    g1z[1].forward()
    g1z[2].send()
    done(g2y[1])
    by_column(col(1), C2)
    g2y[3].forward()
    g2y[2].send()
    w_sdown.wait()
    for xx in range(4):
        S[xx] = jnp.concatenate(
            [jnp.dot(sact, RAW[:, base + 448 * xx:base + 448 * xx + 448], preferred_element_type=F32)
             for base in (0, 1792)], axis=1).astype(BF16)
    g1z[3].forward()
    done(g3x[1])
    done(g1z[1])
    by_row(row(1), RC)
    g2y[2].forward()
    g3x[2].forward()
    done(g2y[3])
    by_column(col(3), C2)
    g1z[2].forward()
    done(g3x[3])
    done(g1z[3])
    by_row(row(3), RC)
    for d in range(1, 16):
        q = (q_me + 16 - d) % 16
        pltpu.make_async_remote_copy(
            src_ref=wt.at[q], dst_ref=WT.at[q], send_sem=wt_send.at[d], recv_sem=wt_recv.at[d],
            device_id=me.plane(q), device_id_type=MESH).wait()

    def finish(yb):
        def body(kb, carry):
            w = jnp.transpose(WT[yb * 4 + kb])
            for n in range(2):
                g = acc[n, yb, kb]
                u = acc[2 + n, yb, kb]
                v = (g / (1.0 + jnp.exp(-g)) * u * w[:, n:n + 1]).astype(BF16)
                hs = pl.ds(n * HID, HID)
                act_a[yb, kb, :, hs] = v[0:48]
                act_b[yb, kb, :, hs] = v[48:96]
                act_c[kb, yb, :, hs] = v[96:128]
            return carry

        lax.fori_loop(0, 4, body, 0)

    done(g2y[2])
    by_column(col(2), C2)
    finish(y)
    finish(row(1))
    finish(row(3))
    done(g1z[2])
    by_row(row(2), C1)
    done(g3x[2])
    by_row(row(2), QC)
    finish(row(2))
    links.wait(swap_down, DW.at[:, pl.ds(HID, HID)], peer)
    links.drain()


class Reduce:
    def __init__(self, links, part, bufs, nb, i, add, add3):
        self.links, self.part, self.bufs, self.nb, self.i = links, part, bufs, nb, i
        self.add, self.add3 = add, add3
        self.s = [links.slot() for _ in range(6)]

    def t(self, d):
        return (self.i + d + 4) % 4

    def first(self):
        l, p, b, s = self.links, self.part, self.bufs, self.s
        l.start(s[0], p(self.t(2), 0), b(0), self.nb(1))
        l.start(s[1], p(self.t(2), 1), b(1), self.nb(-1))

    def second_right(self):
        self.links.start(self.s[2], self.part(self.t(1), 1), self.bufs(2), self.nb(1))

    def second_left(self):
        self.links.start(self.s[3], self.part(self.t(-1), 0), self.bufs(3), self.nb(-1))

    def third(self):
        l, p, b, s = self.links, self.part, self.bufs, self.s
        l.wait(s[0], b(0), self.nb(-1))
        self.add(p(self.t(1), 0), b(0))
        l.start(s[4], p(self.t(1), 0), b(4), self.nb(1))
        l.wait(s[1], b(1), self.nb(1))
        self.add(p(self.t(-1), 1), b(1))
        l.start(s[5], p(self.t(-1), 1), b(5), self.nb(-1))

    def last(self):
        l, p, b, s = self.links, self.part, self.bufs, self.s
        l.wait(s[3], b(3), self.nb(1))
        l.wait(s[4], b(4), self.nb(-1))
        self.add3(p(self.i, 0), b(3), b(4))
        l.wait(s[2], b(2), self.nb(-1))
        l.wait(s[5], b(5), self.nb(1))
        self.add3(p(self.i, 1), b(2), b(5))


def reduce_phase(me, links, act, DW, S, bufs, F, E, G, out, PA, PB, PC):
    x, y, k = me.x, me.y, me.k
    act_a, act_b, act_c = act
    (A1, A2, A3, A4), (B1, B2, B3, B4), (CC1, CC2, CC3, CC4) = bufs

    def add2d(dst, a):
        dst[...] = (dst[...].astype(F32) + a[...].astype(F32)).astype(BF16)

    def add3_2d(dst, a, b):
        dst[...] = (dst[...].astype(F32) + a[...].astype(F32) + b[...].astype(F32)).astype(BF16)

    def add3d(dst, a):
        lax.fori_loop(0, dst.shape[0], lambda n, t: (add2d(dst.at[n], a.at[n]), t)[1], 0)

    def add3_3d(dst, a, b):
        lax.fori_loop(0, dst.shape[0], lambda n, t: (add3_2d(dst.at[n], a.at[n], b.at[n]), t)[1], 0)

    def add4d(dst, a):
        w = dst.shape[1]
        lax.fori_loop(0, dst.shape[0] * w, lambda n, t: (add2d(dst.at[n // w, n % w], a.at[n // w, n % w]), t)[1], 0)

    def add3_4d(dst, a, b):
        w = dst.shape[1]
        lax.fori_loop(
            0, dst.shape[0] * w,
            lambda n, t: (add3_2d(dst.at[n // w, n % w], a.at[n // w, n % w], b.at[n // w, n % w]), t)[1], 0)

    NS = ((0, 256), (256, 256), (512, 256), (768, 128))

    def shared(xx, off, rows):
        return S[xx, off:off + rows, :].astype(F32)

    def down_a(t):
        def body(m, carry):
            lhs = act_a[pl.ds(2 * m, 2)].reshape(8 * 48, 512)
            for lo, w in NS:
                r = jnp.dot(lhs, DW[t, :, lo:lo + w], preferred_element_type=F32)
                PA[t, pl.ds(2 * m, 2), :, :, lo:lo + w] = r.astype(BF16).reshape(2, 4, 48, w)
            return carry
        lax.fori_loop(0, 2, body, 0)
        PA[t, y, k] = (PA[t, y, k].astype(F32) + shared(t, 0, 48)).astype(BF16)

    def down_b(t):
        def body(xx, carry):
            lhs = act_b[t].reshape(4 * 48, 512)
            for lo, w in NS:
                r = jnp.dot(lhs, DW[xx, :, lo:lo + w], preferred_element_type=F32)
                PB[t, :, xx, :, lo:lo + w] = r.astype(BF16).reshape(4, 48, w)
            return carry
        lax.fori_loop(0, 4, body, 0)

    def down_c(t):
        def body(xx, carry):
            lhs = act_c[t].reshape(4 * 32, 512)
            for lo, w in NS:
                r = jnp.dot(lhs, DW[xx, :, lo:lo + w], preferred_element_type=F32)
                PC[t, xx, :, :, lo:lo + w] = r.astype(BF16).reshape(4, 32, w)
            return carry
        lax.fori_loop(0, 4, body, 0)

    def two(h):
        return pl.ds(2 * h, 2)

    def part_rows(p, h):
        return pl.ds(0, SPLIT[p]) if h == 0 else pl.ds(SPLIT[p], ROWS[p] - SPLIT[p])

    def last_bufs(p, pair):
        return lambda n: pair[0].at[n // 2] if n in (0, 3, 4) else pair[1].at[n // 2]

    ra = Reduce(links, lambda t, h: PA.at[t, two(h)], lambda n: A1.at[n], me.xn, x, add4d, add3_4d)
    rb = Reduce(links, lambda t, h: PB.at[t, two(h)], lambda n: B1.at[n], me.yn, y, add4d, add3_4d)
    rc = Reduce(links, lambda t, h: PC.at[t, two(h)], lambda n: CC1.at[n], me.zn, k, add4d, add3_4d)
    down_b((y + 2) % 4)
    rb.first()
    down_a((x + 2) % 4)
    ra.first()
    down_c((k + 2) % 4)
    rc.first()
    down_b((y + 1) % 4)
    rb.second_right()
    down_b((y + 3) % 4)
    rb.second_left()
    down_a((x + 1) % 4)
    ra.second_right()
    down_a((x + 3) % 4)
    ra.second_left()
    down_c((k + 1) % 4)
    rc.second_right()
    down_c((k + 3) % 4)
    rc.second_left()
    rc.third()
    rb.third()
    ra.third()
    down_a(x)
    down_b(y)
    down_c(k)

    def own_shared(xx, carry):
        PB[y, k, xx] = (PB[y, k, xx].astype(F32) + shared(xx, 48, 48)).astype(BF16)
        PC[k, xx, y] = (PC[k, xx, y].astype(F32) + shared(xx, 96, 32)).astype(BF16)
        return carry

    lax.fori_loop(0, 4, own_shared, 0)

    sa = Reduce(links, lambda t, h: PA.at[x, t, two(h)], lambda n: A2.at[n], me.yn, y, add3d, add3_3d)
    sb = Reduce(links, lambda t, h: PB.at[y, t, two(h)], lambda n: B2.at[n], me.zn, k, add3d, add3_3d)
    sc = Reduce(links, lambda t, h: PC.at[k, t, two(h)], lambda n: CC2.at[n], me.xn, x, add3d, add3_3d)
    ta = Reduce(links, lambda t, h: PA.at[x, y, t, part_rows(0, h)], last_bufs(0, (A3, A4)), me.zn, k, add2d, add3_2d)
    tb = Reduce(links, lambda t, h: PB.at[y, k, t, part_rows(1, h)], last_bufs(1, (B3, B4)), me.xn, x, add2d, add3_2d)
    tc = Reduce(links, lambda t, h: PC.at[k, x, t, part_rows(2, h)], last_bufs(2, (CC3, CC4)), me.yn, y, add2d, add3_2d)

    def enter(before, after):
        before.last()
        after.first()
        after.second_right()
        after.second_left()

    enter(rc, sc)
    enter(ra, sa)
    enter(rb, sb)
    sc.third()
    sa.third()
    sb.third()
    enter(sc, tc)
    enter(sa, ta)
    enter(sb, tb)
    tc.third()
    ta.third()
    tb.third()
    low = me.zh == 0
    far = me.zn(4)

    def exchange(own, p, F):
        rows = pl.ds(OFFS[p], ROWS[p])
        whole = own[...]
        lo = whole[:, 0:448].astype(F32)
        hi = whole[:, 448:896].astype(F32)
        E[rows] = jnp.where(low, hi, lo).astype(BF16)
        F[rows] = jnp.where(low, lo, hi)
        slot = links.slot()
        links.start(slot, E.at[rows], G.at[rows], far)
        return slot

    tc.last()
    slot_c = exchange(PC.at[k, x, y], 2, F)
    ta.last()
    slot_a = exchange(PA.at[x, y, k], 0, F)
    tb.last()
    slot_b = exchange(PB.at[y, k, x], 1, F)
    for p, slot in ((2, slot_c), (0, slot_a), (1, slot_b)):
        rows = pl.ds(OFFS[p], ROWS[p])
        links.wait(slot, G.at[rows], far)
        F[rows] = F[rows] + G[rows].astype(F32)
    out[...] = jnp.transpose(F[...]).astype(BF16)
    links.drain()


def layer_body(tokens, ids, rw, swap, gate, up, down, sgate, sup, sdown, out,
               act_a, act_b, act_c, DW, S, A1, A2, A3, A4, B1, B2, B3, B4, CC1, CC2, CC3, CC4, F, E, G,
               send_sem, recv_sem, local_sem, wt_send, wt_recv):
    me = Place()
    links = Links(send_sem, recv_sem)
    act = (act_a, act_b, act_c)
    vmem = pltpu.VMEM
    pl.run_scoped(
        functools.partial(gather_phase, me, links, tokens, ids, rw, swap, gate, up, down, sgate, sup, sdown, act, DW, S,
                          (local_sem, wt_send, wt_recv)),
        vmem((4, 4, TOK, D), BF16), vmem((4, D, HID), BF16), vmem((D, HID), BF16), vmem((HID, D), BF16),
        vmem((4, 4, 4, TOK, HID), F32), vmem((16, 8, TOK), F32), vmem((16, 8, TOK), F32))
    pl.run_scoped(
        functools.partial(reduce_phase, me, links, act, DW, S,
                          ((A1, A2, A3, A4), (B1, B2, B3, B4), (CC1, CC2, CC3, CC4)), F, E, G, out),
        vmem((4, 4, 4, 48, XC), BF16), vmem((4, 4, 4, 48, XC), BF16), vmem((4, 4, 4, 32, XC), BF16))


VM = pl.BlockSpec(memory_space=pltpu.VMEM)
ANY = pl.BlockSpec(memory_space=pl.ANY)


def local(tokens, expert_ids, route_weight, pair_swap, expert_gate, expert_up, expert_down,
          shared_gate, shared_up, shared_down):
    shape = jax.ShapeDtypeStruct
    scratch = pltpu.VMEM
    dma = pltpu.SemaphoreType.DMA
    return pl.pallas_call(
        layer_body,
        name="expert_layer",
        out_shape=shape((448, TOK), BF16),
        in_specs=[ANY, VM, VM, pl.BlockSpec(memory_space=pltpu.SMEM), ANY, ANY, ANY, ANY, ANY, ANY],
        out_specs=VM,
        scratch_shapes=[
            scratch((4, 4, 48, 512), BF16), scratch((4, 4, 48, 512), BF16), scratch((4, 4, 32, 512), BF16),
            scratch((4, 512, XC), BF16), scratch((4, TOK, XC), BF16),
            scratch((6, 2, 4, 48, XC), BF16), scratch((6, 2, 48, XC), BF16),
            scratch((3, 32, XC), BF16), scratch((3, 16, XC), BF16),
            scratch((6, 2, 4, 48, XC), BF16), scratch((6, 2, 48, XC), BF16),
            scratch((3, 32, XC), BF16), scratch((3, 16, XC), BF16),
            scratch((6, 2, 4, 32, XC), BF16), scratch((6, 2, 32, XC), BF16),
            scratch((3, 16, XC), BF16), scratch((3, 16, XC), BF16),
            scratch((TOK, 448), F32), scratch((TOK, 448), BF16), scratch((TOK, 448), BF16),
            dma((192,)), dma((192,)), dma((8,)), dma((16,)), dma((16,)),
        ],
        compiler_params=pltpu.CompilerParams(collective_id=0, has_side_effects=True, vmem_limit_bytes=63 << 20),
    )(tokens, expert_ids.T, route_weight.T, pair_swap, expert_gate[0], expert_up[0], expert_down[0], shared_gate, shared_up, shared_down).T


def solution(mesh):
    in_specs = (
        P("expert", None),
        P("expert", None),
        P("expert", None),
        P(),
        P("expert", None, "dp"),
        P("expert", None, "dp"),
        P("expert", "dp", None),
        P(None, "dp"),
        P(None, "dp"),
        P("dp", None),
    )
    return jax.shard_map(local, mesh=mesh, in_specs=in_specs, out_specs=P("expert", "dp"), check_vma=False)
```
